32 devices in a mesh: grp: 2 (over y), freq: 4 (over z), ell: 2 (over x), pol: 2 (over core).
Axes of the slice: x: 2, y: 2, z: 4, core: 2. Of those that a mesh axis runs over, the one named last changes fastest.
Arguments:
- beam_matrix: bfloat16 [8, 2, 512, 8192], P(('grp', 'freq'), None, None, ('ell', 'pol')), parts along dimension 0, may hold values from -0.375 to 0.375
- sky_spectrum: float32 [8, 3, 8192], P(('grp', 'freq'), None, ('ell', 'pol')), parts along dimension 0, may hold values from 0.1 to 10
- taper_tiles: bfloat16 [3, 512, 512], P(None, ('ell', 'pol')), may hold values from 0.5 to 1.5
- noise_tiles: bfloat16 [8, 3, 512, 2, 512], P(('grp', 'freq'), None, ('ell', 'pol')), parts along dimension 0, may hold values from -4 to 4
Outputs:
- covariance: float32 [8, 3, 512, 2, 512], P(('grp', 'freq'), None, ('ell', 'pol')), parts along dimension 0
The draws below stay inside these ranges and needn't reach their ends.
There are 2 independent parts, one for each index of `grp`. The reference program is written for one: setup_inputs(seed, part) draws one part's arguments, and reference() takes and returns one part's arrays. A program takes and returns all parts, laid end to end along the dimension named above; an argument that names none is the same for every part. Nothing has to cross between parts.
All inputs are finite; a program needn't handle non-finite values.
Results may differ from the reference program's by a relative error of at most 0.012.
Values may be sent and summed in bfloat16 or wider, within the bound.
A program may use at most 64 MiB of HBM per device.

```python
import math
import jax
import jax.numpy as jnp
from jax import lax

MODES = 512
LPOL = 8192
SEPS = 3
NFREQ = 4
N_ELL = 2
N_POL = 2


def raised(array, key, source, target, blocks, factor):
    def block_of(position):
        return (jnp.arange(array.shape[position]) // (array.shape[position] // blocks)).reshape((-1,) + (1,) * (array.ndim - 1 - position))

    near = jax.random.permutation(key, blocks)[block_of(target)]
    other_side = (block_of(target) + blocks // 2) % blocks
    return jnp.where((block_of(source) == near) | (block_of(source) == other_side), factor * array, array)


def block_levels(stream_key, dims, pieces, low, top_value):
    factor_of, own = 1.0, jax.random.fold_in(stream_key, 6)
    for position, parts in pieces:
        draws = jnp.exp(jax.random.uniform(jax.random.fold_in(own, position), (parts,), jnp.float32, low / len(pieces), top_value / len(pieces)))
        factor_of = factor_of * jnp.repeat(draws, dims[position] // parts).reshape([-1 if axis == position else 1 for axis in range(len(dims))])
    return factor_of


def centred(rng, dims, deviation, most, cuts=(), held_as=jnp.bfloat16):
    loudness = block_levels(rng, dims, cuts, -0.22, 0.18) if cuts else 1.0
    values = jax.random.normal(rng, dims, jnp.float32) * deviation * loudness
    return jnp.minimum(jnp.maximum(values, -most), most).astype(held_as)


def bell_draw_with(rng, extent, deviation, reach, cuts, heavy, held_as=jnp.bfloat16):
    drawn = deviation * jax.random.normal(rng, extent, jnp.float32)
    if cuts:
        drawn = drawn * block_levels(rng, extent, cuts, -0.22, 0.18)
    return jnp.clip(raised(drawn, jax.random.fold_in(rng, 3), *heavy), -reach, reach).astype(held_as)


def setup_inputs(seed: int = 0, part: int = 0) -> dict:
    keys = jax.random.split(jax.random.key(seed), 5)
    part_splits = jax.random.split(jax.random.fold_in(keys[4], part), 5)
    beam_matrix = bell_draw_with(part_splits[0], (NFREQ, 2, MODES, LPOL), (LPOL // 16) ** -0.5, 0.375, ((0, 4), (3, 4)), (3, 2, 4, 2.0))
    sky_spectrum = jnp.clip(jnp.exp(math.log(10.0) - 4.6051702 * jax.random.uniform(part_splits[1], (NFREQ, SEPS, LPOL), jnp.float32) ** block_levels(part_splits[1], (NFREQ, SEPS, LPOL), ((0, 4), (2, 4)), -0.2, 0.2)), 0.1, 10.0)
    taper_tiles = jnp.clip(0.5 + 1.0 * jax.random.uniform(keys[2], (SEPS, MODES, MODES), jnp.float32) ** block_levels(keys[2], (SEPS, MODES, MODES), ((1, 4),), -0.2, 0.2), 0.5, 1.5).astype(jnp.bfloat16)
    noise_tiles = centred(part_splits[3], (NFREQ, SEPS, MODES, 2, MODES), 0.5, 4.0, ((0, 4), (2, 4)))
    return dict(beam_matrix=beam_matrix, sky_spectrum=sky_spectrum, taper_tiles=taper_tiles, noise_tiles=noise_tiles)


def tile_sum(own_beam, spec_row, partner):
    mode_count = own_beam.shape[1]
    multipoles = own_beam.shape[2]
    group_count = N_ELL * N_POL
    group_width = multipoles // group_count
    scaled = (spec_row[None, None, :] * own_beam.astype(jnp.float32)).astype(jnp.bfloat16)
    scaled = lax.optimization_barrier(scaled)
    left_wide = scaled.astype(jnp.float32).reshape(2, mode_count, group_count, group_width)
    right_wide = partner.astype(jnp.float32).reshape(2, mode_count, group_count, group_width)
    real_part = jnp.einsum("mgl,ngl->gmn", left_wide[0], right_wide[0]) + jnp.einsum("mgl,ngl->gmn", left_wide[1], right_wide[1])
    imag_part = jnp.einsum("mgl,ngl->gmn", left_wide[1], right_wide[0]) - jnp.einsum("mgl,ngl->gmn", left_wide[0], right_wide[1])
    partials = jnp.stack([real_part, imag_part], axis=2).astype(jnp.bfloat16)
    partials = lax.optimization_barrier(partials)
    return jnp.sum(partials.astype(jnp.float32), axis=0)


def reference(beam_matrix, sky_spectrum, taper_tiles, noise_tiles):
    freq_total = beam_matrix.shape[0]

    def one_freq(bundle):
        own_beam, spec_rows, noise_rows, freq_index = bundle
        per_sep = []
        for sep_index in range(SEPS):
            target = freq_index + sep_index + 1
            picked = jnp.minimum(target, freq_total - 1).astype(jnp.int32)
            partner = lax.dynamic_index_in_dim(beam_matrix, picked, 0, keepdims=False)
            partner = jnp.where(target < freq_total, partner, jnp.zeros_like(partner))
            summed = tile_sum(own_beam, spec_rows[sep_index], partner)
            per_sep.append(taper_tiles[sep_index].astype(jnp.float32)[:, None, :] * summed + noise_rows[sep_index].astype(jnp.float32))
        return jnp.stack(per_sep)

    indices = jnp.arange(freq_total, dtype=jnp.int32)
    return lax.map(one_freq, (beam_matrix, sky_spectrum, noise_tiles, indices))
```

```python
import functools

import jax
import jax.numpy as jnp
from jax import lax
from jax.experimental import pallas as pl
from jax.experimental.pallas import tpu as pltpu
from jax.sharding import PartitionSpec as P

FINE = 8
COARSE = 4
LATE = 2
LANES = 128


def passed_along(block, axis, distance):
    devices = range(lax.axis_size(axis))
    route = [(i - distance, i) for i in devices if i - distance in devices]
    return lax.ppermute(block, axis, route)


def general_sums(beam_matrix, sky_spectrum, local_rows):
    per_device = beam_matrix.shape[0]
    mode_count = beam_matrix.shape[2]
    separations = sky_spectrum.shape[1]
    needed = (per_device - 1 + separations) // per_device
    blocks = [beam_matrix]
    for offset in range(needed):
        blocks.append(passed_along(beam_matrix, "freq", -(offset + 1)))
    term_list = []
    for sep_index in range(separations):
        target = sep_index + 1
        partner = blocks[target // per_device][target % per_device]
        spec_row = sky_spectrum[0, sep_index]
        scaled = (spec_row[None, None, :] * beam_matrix[0].astype(jnp.float32)).astype(jnp.bfloat16)
        right = jnp.concatenate([partner[0], partner[1]], axis=-1)
        top = jnp.concatenate([scaled[0], scaled[1]], axis=-1)
        bottom = jnp.concatenate([scaled[1], -scaled[0]], axis=-1)
        left = jnp.stack([top, bottom], axis=1).reshape(2 * mode_count, top.shape[-1])
        product = lax.dot_general(
            left, right, (((1,), (1,)), ((), ())), preferred_element_type=jnp.float32
        ).reshape(mode_count, 2, mode_count)
        term_list.append(
            lax.psum_scatter(
                product.astype(jnp.bfloat16), ("ell", "pol"), scatter_dimension=0, tiled=True
            ).astype(jnp.float32)
        )
    return jnp.stack(term_list)


S0, S1, S2, S3 = range(4)


def meet_kernel(
    cut, own_hbm, spec, taper, out,
    own, outer, near, far, spec0, spec1, stage, inbox, back_out, back_in, final_out, final_in,
    load, spec_s, spec_r, hi_s, hi_r, lo_s, lo_r, mid_s, mid_r, nr_s, nr_r, fr_s, fr_r, fl_s, fl_r,
    rs_s, rs_r, bk_s, bk_r, fn_s, fn_r,
):
    f32, bf16 = jnp.float32, jnp.bfloat16
    _, groups, rows, width = own.shape
    modes = groups * rows
    fine, coarse, halves = FINE, COARSE, 2
    few = fine - LATE
    freqs = lax.axis_size("freq")
    pols = lax.axis_size("pol")
    freq = lax.axis_index("freq")
    me = lax.axis_index("ell") * pols + lax.axis_index("pol")
    low, high, full = (0, cut), (cut, width), (0, width)
    every = slice(None)
    per_row = 2 * modes // LANES

    loading = pltpu.make_async_copy(own_hbm, own, load)
    loading.start()

    barrier = pltpu.get_barrier_semaphore()
    for d in range(1, freqs):
        pl.semaphore_signal(
            barrier, inc=1, device_id={"freq": lax.rem(freq + d, freqs)},
            device_id_type=pl.DeviceIdType.MESH,
        )
    for d in range(1, groups):
        other = lax.rem(me + d, groups)
        pl.semaphore_signal(
            barrier, inc=1, device_id={"ell": other // pols, "pol": lax.rem(other, pols)},
            device_id_type=pl.DeviceIdType.MESH,
        )
    pl.semaphore_wait(barrier, freqs - 1 + groups - 1)

    def span(c, pieces):
        step = rows // pieces
        return pl.ds(pl.multiple_of(c * step, step), step)

    def to_freq(src, dst, send, recv, target):
        return pltpu.make_async_remote_copy(
            src_ref=src, dst_ref=dst, send_sem=send, recv_sem=recv,
            device_id={"freq": target}, device_id_type=pl.DeviceIdType.MESH,
        )

    def lanes(part):
        return pl.ds(part[0], part[1] - part[0])

    def loop(lo, hi, body):
        def wrapped(i, carry):
            body(i)
            return carry

        lax.fori_loop(lo, hi, wrapped, 0)

    def send_spec(dst, n, target):
        which = 0 if dst is spec0 else 1
        return to_freq(spec, dst, spec_s.at[n], spec_r.at[which], target)

    def moved(src, dst, where, send, recv, target):
        return to_freq(src.at[where], dst.at[where], send, recv, target)

    def row_piece(c, pieces, part):
        return (every, every, span(c, pieces), lanes(part))

    def block_piece(g, count, part):
        return (every, pl.ds(g * count, count), every, lanes(part))

    def outer_high(c):
        return moved(own_hbm, outer, row_piece(c, fine, high), hi_s.at[c], hi_r.at[c], 1)

    def outer_low(c):
        return moved(own_hbm, outer, row_piece(c, coarse, low), lo_s.at[c], lo_r.at[c], 1)

    def first_on(src, c, target):
        return moved(src, near, row_piece(c, fine, high), nr_s.at[c], nr_r.at[c], target)

    def second_on(src, c, target):
        return moved(src, far, row_piece(c, fine, high), fr_s.at[c], fr_r.at[c], target)

    def last_low(g):
        return moved(own_hbm, outer, block_piece(g, 1, low), lo_s.at[g], lo_r.at[g], 2)

    def last_high(g):
        return moved(
            own_hbm, outer, block_piece(g, groups // halves, high), hi_s.at[g], hi_r.at[g], 2
        )

    def last_on(g):
        return moved(outer, far, block_piece(g, 1, low), fl_s.at[g], fl_r.at[g], 1)

    def third_on(src, g, target):
        return moved(src, near, block_piece(g, 1, low), mid_s.at[g], mid_r.at[g], target)

    def share(slot, piece, where):
        copies = []
        for d in range(1, groups):
            other = lax.rem(me + d, groups)
            copies.append(
                pltpu.make_async_remote_copy(
                    src_ref=stage.at[(slot, other) + where],
                    dst_ref=inbox.at[(slot, d - 1) + where],
                    send_sem=rs_s.at[slot, piece, d - 1],
                    recv_sem=rs_r.at[slot, piece, d - 1],
                    device_id={"ell": other // pols, "pol": lax.rem(other, pols)},
                    device_id_type=pl.DeviceIdType.MESH,
                )
            )
        return copies

    def start_share(slot, piece, where):
        for copy in share(slot, piece, where):
            copy.start()

    def rows_of(c, pieces):
        return (every, span(c, pieces), every)

    def cols_of(g):
        size = modes // halves
        return (every, every, pl.ds(pl.multiple_of(g * size, size), size))

    def dot(a, b):
        return lax.dot_general(a, b, (((1,), (1,)), ((), ())), preferred_element_type=f32)

    def cross(left, left_where, weight, right, right_where):
        def scaled(part_index):
            value = left[(part_index,) + left_where].reshape(-1, weight.shape[-1])
            return (weight * value.astype(f32)).astype(bf16)

        a_re, a_im = scaled(0), scaled(1)
        b_re = right[(0,) + right_where].reshape(-1, weight.shape[-1])
        b_im = right[(1,) + right_where].reshape(-1, weight.shape[-1])
        both = dot(jnp.concatenate([a_re, a_im], 0), b_re)
        both = both + dot(jnp.concatenate([a_im, -a_re], 0), b_im)
        size = a_re.shape[0]
        return both[:size].astype(bf16), both[size:].astype(bf16)

    def by_rows(slot, c, pieces, left, weights, sep, right, part):
        weight = weights[sep, :, lanes(part)]
        real, imag = cross(
            left, (every, span(c, pieces), lanes(part)), weight, right, (every, every, lanes(part))
        )
        stage[slot, :, 0, span(c, pieces), :] = real.reshape(groups, rows // pieces, modes)
        stage[slot, :, 1, span(c, pieces), :] = imag.reshape(groups, rows // pieces, modes)
        start_share(slot, c, rows_of(c, pieces))

    def by_columns(slot, g, left, weights, sep, right, part):
        weight = weights[sep, :, lanes(part)]
        count = groups // halves
        columns = cols_of(g)[-1]

        def body(o):
            real, imag = cross(
                left, (o, every, lanes(part)), weight,
                right, (pl.ds(g * count, count), every, lanes(part)),
            )
            stage[slot, o, 0, :, columns] = real
            stage[slot, o, 1, :, columns] = imag

        loop(0, groups, body)
        start_share(slot, g, cols_of(g))

    def await_share(slot, piece, where):
        for copy in share(slot, piece, where):
            copy.wait_recv()

    def added(slot, where):
        total = stage[(slot, me) + where].astype(f32)
        for d in range(groups - 1):
            total = total + inbox[(slot, d) + where].astype(f32)
        return total

    def settle(slot, pieces, where_of, lo=0):
        def body(c):
            for copy in share(slot, c, where_of(c)):
                copy.wait_send()

        loop(lo, pieces, body)

    def fine_rows(c):
        return rows_of(c, fine)

    def coarse_rows(c):
        return rows_of(c, coarse)

    def give_back(slot, c):
        where = fine_rows(c)
        return to_freq(
            back_out.at[(slot,) + where], back_in.at[(slot,) + where],
            bk_s.at[slot, c], bk_r.at[slot, c], 0 if slot in (S0, S3) else 1,
        )

    def returned(slot):
        def body(c):
            where = fine_rows(c)
            await_share(slot, c, where)
            back_out[(slot,) + where] = added(slot, where).astype(bf16)
            give_back(slot, c).start()

        return body

    def deliver(n, c):
        where = coarse_rows(c)
        return to_freq(
            final_out.at[(n,) + where], final_in.at[(n,) + where], fn_s.at[n, c], fn_r.at[n, c], 0
        )

    def delivered(slot, n):
        def body(c):
            where = coarse_rows(c)
            await_share(slot, c, where)
            final_out[(n,) + where] = added(slot, where).astype(bf16)
            deliver(n, c).start()

        return body

    def finish(sep, first_row, count, first_block, total):
        weight = taper[sep, pl.ds(first_row, count), pl.ds(first_block * LANES, total.shape[-1])]
        weight = weight.astype(f32)
        for part in range(2):
            value = weight * total[part]
            for j in range(total.shape[-1] // LANES):
                start = first_row * per_row + 2 * (first_block + j) + part
                out[sep, pl.ds(start, count, stride=per_row), :] = value[
                    :, j * LANES:(j + 1) * LANES
                ]

    def finish_rows(sep, c, pieces, total):
        step = rows // pieces
        finish(sep, pl.multiple_of(c * step, step), step, 0, total)

    def clear(sep):
        out[sep] = jnp.zeros(out.shape[1:], f32)

    @pl.when(freq == 0)
    def _():
        for n in range(1, freqs):
            send_spec(spec0, n - 1, n).start()
        loop(0, fine, lambda c: outer_high(c).start())
        loop(0, coarse, lambda c: outer_low(c).start())
        loading.wait()
        loop(0, groups, lambda g: third_on(near, g, 0).wait_recv())
        loop(0, coarse, lambda c: by_rows(S0, c, coarse, own, spec, 1, near, low))
        loop(0, coarse, lambda c: await_share(S0, c, coarse_rows(c)))

        def ends(c):
            deliver(0, c).wait_recv()
            finish_rows(0, c, coarse, final_in[(0,) + coarse_rows(c)].astype(f32))

        def middles(c):
            where = fine_rows(c)
            give_back(S0, c).wait_recv()
            finish_rows(1, c, fine, added(S0, where) + back_in[(S0,) + where].astype(f32))

        def longs(c):
            per = fine // coarse
            where = fine_rows(c)

            @pl.when(lax.rem(c, per) == 0)
            def _():
                deliver(1, c // per).wait_recv()

            give_back(S3, c).wait_recv()
            total = final_in[(1,) + where].astype(f32) + back_in[(S3,) + where].astype(f32)
            finish_rows(2, c, fine, total)

        loop(0, coarse - 1, ends)
        loop(0, fine, middles)
        loop(coarse - 1, coarse, ends)
        loop(0, fine, longs)
        for n in range(1, freqs):
            send_spec(spec0, n - 1, n).wait_send()
        loop(0, fine, lambda c: outer_high(c).wait_send())
        loop(0, coarse, lambda c: outer_low(c).wait_send())
        settle(S0, coarse, coarse_rows)

    @pl.when(freq == 1)
    def _():
        for n in range(2):
            second_on(own_hbm, n, 2).start()
            send_spec(spec1, n, n + 2).start()
        clear(2)

        def relay(c):
            outer_high(c).wait_recv()
            first_on(outer, c, 2).start()

        def relay_back(g):
            third_on(own_hbm, g, 1).wait_recv()
            third_on(near, g, 0).start()

        done = 0
        for c in range(fine):
            relay(c)
            while done < groups and 2 * fine * (done + 1) <= groups * (2 * c + 3):
                relay_back(done)
                done += 1
        for g in range(done, groups):
            relay_back(g)
        loop(2, fine, lambda c: second_on(own_hbm, c, 2).start())
        loading.wait()
        send_spec(spec0, 0, 1).wait_recv()
        loop(0, coarse, lambda c: by_rows(S1, c, coarse, own, spec, 0, near, low))

        def take(c):
            outer_low(c).wait_recv()
            by_rows(S0, c, coarse, outer, spec0, 0, own, full)

            @pl.when(c == coarse - 2)
            def _():
                loop(0, groups, lambda g: last_on(g).wait_recv())
                loop(0, coarse, lambda r: by_rows(S2, r, coarse, own, spec, 1, far, low))

            @pl.when(c >= coarse - 2)
            def _():
                loop(
                    jnp.where(c == coarse - 2, 0, c), c + 1,
                    lambda r: by_rows(S3, r, coarse, outer, spec0, 2, far, low),
                )

            loop(jnp.maximum(c - 1, 0), c, delivered(S0, 0))
            loop(0, jnp.where(c == coarse - 1, c, 0), delivered(S3, 1))

        loop(0, coarse, take)
        loop(coarse - 1, coarse, delivered(S0, 0))
        loop(coarse - 1, coarse, delivered(S3, 1))
        loop(0, coarse, lambda c: await_share(S1, c, coarse_rows(c)))
        loop(0, coarse, lambda c: await_share(S2, c, coarse_rows(c)))

        def ends(slot, sep):
            def body(c):
                where = fine_rows(c)
                give_back(slot, c).wait_recv()
                finish_rows(sep, c, fine, added(slot, where) + back_in[(slot,) + where].astype(f32))

            return body

        loop(0, few, ends(S1, 0))
        loop(0, few, ends(S2, 1))

        def late(c):
            ends(S1, 0)(c)
            ends(S2, 1)(c)

        loop(few, fine, late)
        for n in range(2):
            send_spec(spec1, n, n + 2).wait_send()
        loop(0, fine, lambda c: second_on(own_hbm, c, 2).wait_send())
        loop(0, fine, lambda c: first_on(outer, c, 2).wait_send())
        loop(0, groups, lambda g: third_on(near, g, 0).wait_send())
        for slot in range(4):
            settle(slot, coarse, coarse_rows)
        for n in range(2):
            loop(0, coarse, lambda c: deliver(n, c).wait_send())

    @pl.when(freq == 2)
    def _():
        loop(0, groups, lambda g: third_on(own_hbm, g, 1).start())
        clear(1)
        clear(2)
        loading.wait()
        send_spec(spec0, 1, 2).wait_recv()
        send_spec(spec1, 0, 2).wait_recv()

        def second(c):
            second_on(own_hbm, c, 2).wait_recv()
            second_on(far, c, 3).start()
            by_rows(S1, c, fine, far, spec1, 0, own, high)

        def first(c):
            first_on(outer, c, 2).wait_recv()
            first_on(near, c, 3).start()

            @pl.when(c < groups)
            def _():
                last_low(c).wait_recv()
                last_on(c).start()

            by_rows(S0, c, fine, near, spec0, 1, own, high)
            loop(jnp.maximum(c - 1, 0), c, returned(S0))

        def block(g):
            last_high(g).wait_recv()
            by_columns(S3, g, own, spec, 0, outer, full)

        loop(0, 2, second)
        loop(0, 1, returned(S1))
        loop(0, fine, first)
        loop(1, 2, returned(S1))

        def second_more(c):
            second(c)
            loop(c - 1, jnp.where(c > 2, c, c - 1), returned(S1))
            loop(fine - 1, jnp.where(c == 2, fine, fine - 1), returned(S0))
            loop(0, jnp.where(c == 2, 1, 0), block)

        loop(2, few, second_more)
        loop(few - 1, few, returned(S1))
        loop(1, halves, block)

        def tail(c):
            second_on(own_hbm, c, 2).wait_recv()
            by_rows(S1, c, fine, far, spec1, 0, own, high)
            by_rows(S2, c, fine, far, spec1, 1, outer, high)
            returned(S1)(c)
            returned(S2)(c)

        loop(few, fine, tail)
        for g in range(halves):
            where = cols_of(g)
            await_share(S3, g, where)
            size = modes // halves
            finish(0, 0, rows, g * size // LANES, added(S3, where))

        loop(0, groups, lambda g: third_on(own_hbm, g, 1).wait_send())
        loop(0, groups, lambda g: last_on(g).wait_send())
        loop(0, fine, lambda c: first_on(near, c, 3).wait_send())
        loop(0, few, lambda c: second_on(far, c, 3).wait_send())
        settle(S0, fine, fine_rows)
        settle(S1, fine, fine_rows)
        settle(S2, fine, fine_rows, few)
        settle(S3, halves, cols_of)
        loop(0, fine, lambda c: give_back(S0, c).wait_send())
        loop(0, fine, lambda c: give_back(S1, c).wait_send())
        loop(few, fine, lambda c: give_back(S2, c).wait_send())

    @pl.when(freq == 3)
    def _():
        loop(0, groups, lambda g: last_low(g).start())
        loop(0, halves, lambda g: last_high(g).start())
        for sep in range(3):
            clear(sep)
        loading.wait()
        send_spec(spec0, 2, 3).wait_recv()
        send_spec(spec1, 1, 3).wait_recv()

        def second(c):
            second_on(far, c, 3).wait_recv()
            by_rows(S2, c, fine, far, spec1, 1, own, high)
            returned(S2)(c)

        def first(c):
            first_on(near, c, 3).wait_recv()
            by_rows(S3, c, fine, near, spec0, 2, own, high)
            returned(S3)(c)

        loop(0, 2, second)
        loop(0, fine, first)
        loop(2, few, second)
        loop(0, groups, lambda g: last_low(g).wait_send())
        loop(0, halves, lambda g: last_high(g).wait_send())
        settle(S3, fine, fine_rows)
        settle(S2, few, fine_rows)
        loop(0, fine, lambda c: give_back(S3, c).wait_send())
        loop(0, few, lambda c: give_back(S2, c).wait_send())


def meet_covariance(beam_matrix, sky_spectrum, taper_tiles):
    _, parts, modes, width = beam_matrix.shape
    separations, local_rows, _ = taper_tiles.shape
    groups = modes // local_rows
    tiles = 4 * 2 * local_rows * modes
    block = parts * modes * width
    cut = int(width * (0.5 - tiles / (4 * block))) // LANES * LANES
    bf16, f32 = jnp.bfloat16, jnp.float32
    shape = (parts, groups, local_rows, width)
    tile = (2, local_rows, modes)
    blocks = modes // LANES
    dma = pltpu.SemaphoreType.DMA
    pair = lambda *dims: [dma(dims), dma(dims)]
    vmem = pl.BlockSpec(memory_space=pltpu.VMEM)
    spec = jnp.swapaxes(sky_spectrum, 0, 1)
    lines = pl.pallas_call(
        functools.partial(meet_kernel, cut),
        out_shape=jax.ShapeDtypeStruct((separations, local_rows * blocks * 2, LANES), f32),
        in_specs=[pl.BlockSpec(memory_space=pl.ANY), vmem, vmem],
        out_specs=vmem,
        scratch_shapes=[
            *[pltpu.VMEM(shape, bf16)] * 4,
            *[pltpu.VMEM(spec.shape, f32)] * 2,
            pltpu.VMEM((4, groups) + tile, bf16),
            pltpu.VMEM((4, groups - 1) + tile, bf16),
            *[pltpu.VMEM((4,) + tile, bf16)] * 2,
            *[pltpu.VMEM((2,) + tile, bf16)] * 2,
            dma, *pair(3), *pair(FINE), *pair(max(COARSE, groups)), *pair(groups),
            *pair(FINE), *pair(FINE), *pair(groups),
            *pair(4, FINE, groups - 1), *pair(4, FINE), *pair(2, COARSE),
        ],
        compiler_params=pltpu.CompilerParams(
            collective_id=0, has_side_effects=True, vmem_limit_bytes=60 * 2**20
        ),
    )(beam_matrix[0].reshape(shape), spec, taper_tiles)
    lines = lines.reshape(1, separations, local_rows, blocks, 2, LANES)
    return jnp.swapaxes(lines, 3, 4).reshape(1, separations, local_rows, 2, modes)


def local(beam_matrix, sky_spectrum, taper_tiles, noise_tiles):
    per_device, _, modes, width = beam_matrix.shape
    separations = sky_spectrum.shape[1]
    local_rows = taper_tiles.shape[1]
    in_line = (
        per_device == 1
        and separations == 3
        and lax.axis_size("freq") == separations + 1
        and modes // local_rows == 4
        and local_rows % LANES == 0
        and width % (8 * LANES) == 0
    )
    noise = noise_tiles.astype(jnp.float32)
    if in_line:
        return meet_covariance(beam_matrix, sky_spectrum, taper_tiles) + noise
    summed = general_sums(beam_matrix, sky_spectrum, local_rows)
    summed = summed.reshape(per_device, separations, local_rows, 2, modes)
    taper = taper_tiles.astype(jnp.float32)[None, :, :, None, :]
    return taper * summed + noise


def solution(mesh):
    placed = (
        P(("grp", "freq"), None, None, ("ell", "pol")),
        P(("grp", "freq"), None, ("ell", "pol")),
        P(None, ("ell", "pol"), None),
        P(("grp", "freq"), None, ("ell", "pol"), None, None),
    )
    return jax.shard_map(
        local,
        mesh=mesh,
        in_specs=placed,
        out_specs=P(("grp", "freq"), None, ("ell", "pol"), None, None),
        check_vma=False,
    )
```

```python
import functools

import jax
import jax.numpy as jnp
from jax import lax
from jax.experimental import pallas as pl
from jax.experimental.pallas import tpu as pltpu
from jax.sharding import PartitionSpec as P

FINE = 8
COARSE = 4
LATE = 2
LANES = 128


def passed_along(block, axis, distance):
    devices = range(lax.axis_size(axis))
    route = [(i - distance, i) for i in devices if i - distance in devices]
    return lax.ppermute(block, axis, route)


def general_sums(beam_matrix, sky_spectrum, local_rows):
    per_device = beam_matrix.shape[0]
    mode_count = beam_matrix.shape[2]
    separations = sky_spectrum.shape[1]
    needed = (per_device - 1 + separations) // per_device
    blocks = [beam_matrix]
    for offset in range(needed):
        blocks.append(passed_along(beam_matrix, "freq", -(offset + 1)))
    term_list = []
    for sep_index in range(separations):
        target = sep_index + 1
        partner = blocks[target // per_device][target % per_device]
        spec_row = sky_spectrum[0, sep_index]
        scaled = (spec_row[None, None, :] * beam_matrix[0].astype(jnp.float32)).astype(jnp.bfloat16)
        right = jnp.concatenate([partner[0], partner[1]], axis=-1)
        top = jnp.concatenate([scaled[0], scaled[1]], axis=-1)
        bottom = jnp.concatenate([scaled[1], -scaled[0]], axis=-1)
        left = jnp.stack([top, bottom], axis=1).reshape(2 * mode_count, top.shape[-1])
        product = lax.dot_general(
            left, right, (((1,), (1,)), ((), ())), preferred_element_type=jnp.float32
        ).reshape(mode_count, 2, mode_count)
        term_list.append(
            lax.psum_scatter(
                product.astype(jnp.bfloat16), ("ell", "pol"), scatter_dimension=0, tiled=True
            ).astype(jnp.float32)
        )
    return jnp.stack(term_list)


S0, S1, S2, S3 = range(4)


def meet_kernel(
    cut, own_hbm, spec, taper_hbm, out,
    own, taper, outer, near, far, spec0, spec1, stage, inbox, back_out, back_in, final_out, final_in,
    load, load_taper, spec_s, spec_r, hi_s, hi_r, lo_s, lo_r, mid_s, mid_r, nr_s, nr_r, fr_s, fr_r, fl_s, fl_r,
    rs_s, rs_r, bk_s, bk_r, fn_s, fn_r,
):
    f32, bf16 = jnp.float32, jnp.bfloat16
    _, groups, rows, width = own.shape
    modes = groups * rows
    fine, coarse, halves = FINE, COARSE, 2
    held = groups // halves
    few = fine - LATE
    freqs = lax.axis_size("freq")
    pols = lax.axis_size("pol")
    freq = lax.axis_index("freq")
    me = lax.axis_index("ell") * pols + lax.axis_index("pol")
    low, high, full = (0, cut), (cut, width), (0, width)
    every = slice(None)
    per_row = 2 * modes // LANES

    loading = pltpu.make_async_copy(own_hbm, own, load)
    loading.start()
    tapers = pltpu.make_async_copy(taper_hbm, taper, load_taper)
    tapers.start()

    barrier = pltpu.get_barrier_semaphore()
    for d in range(1, freqs):
        pl.semaphore_signal(
            barrier, inc=1, device_id={"freq": lax.rem(freq + d, freqs)},
            device_id_type=pl.DeviceIdType.MESH,
        )
    for d in range(1, groups):
        other = lax.rem(me + d, groups)
        pl.semaphore_signal(
            barrier, inc=1, device_id={"ell": other // pols, "pol": lax.rem(other, pols)},
            device_id_type=pl.DeviceIdType.MESH,
        )
    pl.semaphore_wait(barrier, freqs - 1 + groups - 1)

    def span(c, pieces):
        step = rows // pieces
        return pl.ds(pl.multiple_of(c * step, step), step)

    def to_freq(src, dst, send, recv, target):
        return pltpu.make_async_remote_copy(
            src_ref=src, dst_ref=dst, send_sem=send, recv_sem=recv,
            device_id={"freq": target}, device_id_type=pl.DeviceIdType.MESH,
        )

    def lanes(part):
        return pl.ds(part[0], part[1] - part[0])

    def loop(lo, hi, body):
        def wrapped(i, carry):
            body(i)
            return carry

        lax.fori_loop(lo, hi, wrapped, 0)

    def send_spec(dst, sep, part, n, target):
        where = (pl.ds(sep, 1), every, lanes(part))
        return to_freq(spec.at[where], dst.at[where], spec_s.at[n], spec_r.at[n], target)

    def own_first():
        return [
            send_spec(spec0, 0, full, 0, 1), send_spec(spec0, 1, high, 1, 2),
            send_spec(spec0, 2, high, 2, 3), send_spec(spec0, 2, low, 3, 1),
        ]

    def own_second():
        return [
            send_spec(spec1, 0, high, 4, 2), send_spec(spec1, 1, high, 5, 3),
            send_spec(spec1, 1, high, 6, 2),
        ]

    def moved(src, dst, where, send, recv, target):
        return to_freq(src.at[where], dst.at[where], send, recv, target)

    def row_piece(c, pieces, part):
        return (every, every, span(c, pieces), lanes(part))

    def block_piece(g, count, part):
        return (every, pl.ds(g * count, count), every, lanes(part))

    def outer_high(c):
        return moved(own_hbm, outer, row_piece(c, fine, high), hi_s.at[c], hi_r.at[c], 1)

    def outer_low(c):
        return moved(own_hbm, outer, row_piece(c, coarse, low), lo_s.at[c], lo_r.at[c], 1)

    def first_on(src, c, target):
        return moved(src, near, row_piece(c, fine, high), nr_s.at[c], nr_r.at[c], target)

    def second_on(src, c, target):
        return moved(src, far, row_piece(c, fine, high), fr_s.at[c], fr_r.at[c], target)

    def last_low(g):
        return moved(own_hbm, outer, block_piece(g, 1, low), lo_s.at[g], lo_r.at[g], 2)

    def last_high(g):
        return moved(own_hbm, outer, block_piece(g, 1, high), hi_s.at[g], hi_r.at[g], 2)

    def last_on(g):
        return moved(outer, far, block_piece(g, 1, low), fl_s.at[g], fl_r.at[g], 1)

    def third_on(src, g, target):
        return moved(src, near, block_piece(g, 1, low), mid_s.at[g], mid_r.at[g], target)

    def share(slot, piece, where):
        copies = []
        for d in range(1, groups):
            other = lax.rem(me + d, groups)
            copies.append(
                pltpu.make_async_remote_copy(
                    src_ref=stage.at[(slot, other) + where],
                    dst_ref=inbox.at[(slot, d - 1) + where],
                    send_sem=rs_s.at[slot, piece, d - 1],
                    recv_sem=rs_r.at[slot, piece, d - 1],
                    device_id={"ell": other // pols, "pol": lax.rem(other, pols)},
                    device_id_type=pl.DeviceIdType.MESH,
                )
            )
        return copies

    def start_share(slot, piece, where):
        for copy in share(slot, piece, where):
            copy.start()

    def rows_of(c, pieces):
        return (every, span(c, pieces), every)

    def cols_of(g, count=1):
        size = count * rows
        return (every, every, pl.ds(pl.multiple_of(g * size, size), size))

    def wide_cols(g):
        return cols_of(g, held)

    def dot(a, b):
        return lax.dot_general(a, b, (((1,), (1,)), ((), ())), preferred_element_type=f32)

    def cross(left, left_where, weight, right, right_where):
        def scaled(part_index):
            value = left[(part_index,) + left_where].reshape(-1, weight.shape[-1])
            return (weight * value.astype(f32)).astype(bf16)

        a_re, a_im = scaled(0), scaled(1)
        b_re = right[(0,) + right_where].reshape(-1, weight.shape[-1])
        b_im = right[(1,) + right_where].reshape(-1, weight.shape[-1])
        both = dot(jnp.concatenate([a_re, a_im], 0), b_re)
        both = both + dot(jnp.concatenate([a_im, -a_re], 0), b_im)
        size = a_re.shape[0]
        return both[:size].astype(bf16), both[size:].astype(bf16)

    def by_rows(slot, c, pieces, left, weights, sep, right, part):
        weight = weights[sep, :, lanes(part)]
        real, imag = cross(
            left, (every, span(c, pieces), lanes(part)), weight, right, (every, every, lanes(part))
        )
        stage[slot, :, 0, span(c, pieces), :] = real.reshape(groups, rows // pieces, modes)
        stage[slot, :, 1, span(c, pieces), :] = imag.reshape(groups, rows // pieces, modes)
        start_share(slot, c, rows_of(c, pieces))

    def by_columns(slot, g, count, left, weights, sep, right, part):
        weight = weights[sep, :, lanes(part)]
        columns = cols_of(g, count)[-1]

        def body(o):
            real, imag = cross(
                left, (o, every, lanes(part)), weight,
                right, (pl.ds(g * count, count), every, lanes(part)),
            )
            stage[slot, o, 0, :, columns] = real
            stage[slot, o, 1, :, columns] = imag

        loop(0, groups, body)
        start_share(slot, g, cols_of(g, count))

    def await_share(slot, piece, where):
        for copy in share(slot, piece, where):
            copy.wait_recv()

    def added(slot, where):
        total = stage[(slot, me) + where].astype(f32)
        for d in range(groups - 1):
            total = total + inbox[(slot, d) + where].astype(f32)
        return total

    def settle(slot, pieces, where_of, lo=0):
        def body(c):
            for copy in share(slot, c, where_of(c)):
                copy.wait_send()

        loop(lo, pieces, body)

    def fine_rows(c):
        return rows_of(c, fine)

    def coarse_rows(c):
        return rows_of(c, coarse)

    def give_back(slot, c):
        where = fine_rows(c)
        return to_freq(
            back_out.at[(slot,) + where], back_in.at[(slot,) + where],
            bk_s.at[slot, c], bk_r.at[slot, c], 0 if slot in (S0, S3) else 1,
        )

    def returned(slot):
        def body(c):
            where = fine_rows(c)
            await_share(slot, c, where)
            back_out[(slot,) + where] = added(slot, where).astype(bf16)
            give_back(slot, c).start()

        return body

    def deliver(n, c):
        where = coarse_rows(c)
        return to_freq(
            final_out.at[(n,) + where], final_in.at[(n,) + where], fn_s.at[n, c], fn_r.at[n, c], 0
        )

    def delivered(slot, n):
        def body(c):
            where = coarse_rows(c)
            await_share(slot, c, where)
            final_out[(n,) + where] = added(slot, where).astype(bf16)
            deliver(n, c).start()

        return body

    def finish(sep, first_row, count, first_block, total):
        weight = taper[sep, pl.ds(first_row, count), pl.ds(first_block * LANES, total.shape[-1])]
        weight = weight.astype(f32)
        for part in range(2):
            value = weight * total[part]
            for j in range(total.shape[-1] // LANES):
                start = first_row * per_row + 2 * (first_block + j) + part
                out[sep, pl.ds(start, count, stride=per_row), :] = value[
                    :, j * LANES:(j + 1) * LANES
                ]

    def finish_rows(sep, c, pieces, total):
        step = rows // pieces
        finish(sep, pl.multiple_of(c * step, step), step, 0, total)

    def clear(sep):
        out[sep] = jnp.zeros(out.shape[1:], f32)

    @pl.when(freq == 0)
    def _():
        outer_high(0).start()
        for copy in own_first():
            copy.start()
        loop(1, fine, lambda c: outer_high(c).start())
        loop(0, coarse, lambda c: outer_low(c).start())
        loading.wait()
        tapers.wait()
        loop(0, groups, lambda g: third_on(near, g, 0).wait_recv())
        loop(0, coarse, lambda c: by_rows(S0, c, coarse, own, spec, 1, near, low))
        loop(0, coarse, lambda c: await_share(S0, c, coarse_rows(c)))

        def ends(c):
            deliver(0, c).wait_recv()
            finish_rows(0, c, coarse, final_in[(0,) + coarse_rows(c)].astype(f32))

        def middles(c):
            where = fine_rows(c)
            give_back(S0, c).wait_recv()
            finish_rows(1, c, fine, added(S0, where) + back_in[(S0,) + where].astype(f32))

        def longs(c):
            per = fine // coarse
            where = fine_rows(c)

            @pl.when(lax.rem(c, per) == 0)
            def _():
                deliver(1, c // per).wait_recv()

            give_back(S3, c).wait_recv()
            total = final_in[(1,) + where].astype(f32) + back_in[(S3,) + where].astype(f32)
            finish_rows(2, c, fine, total)

        loop(0, coarse - 1, ends)
        loop(0, fine, middles)
        loop(coarse - 1, coarse, ends)
        loop(0, fine, longs)
        for copy in own_first():
            copy.wait_send()
        loop(0, fine, lambda c: outer_high(c).wait_send())
        loop(0, coarse, lambda c: outer_low(c).wait_send())
        settle(S0, coarse, coarse_rows)

    @pl.when(freq == 1)
    def _():
        second_on(own_hbm, 0, 2).start()
        for copy in own_second():
            copy.start()
        second_on(own_hbm, 1, 2).start()
        clear(2)

        def relay(c):
            outer_high(c).wait_recv()
            first_on(outer, c, 2).start()

        def relay_back(g):
            third_on(own_hbm, g, 1).wait_recv()
            third_on(near, g, 0).start()

        done = 0
        for c in range(fine):
            relay(c)
            while done < groups and 2 * fine * (done + 1) <= groups * (2 * c + 3):
                relay_back(done)
                done += 1
        for g in range(done, groups):
            relay_back(g)
        loop(2, fine, lambda c: second_on(own_hbm, c, 2).start())
        loading.wait()
        tapers.wait()
        own_first()[0].wait_recv()
        own_first()[3].wait_recv()
        loop(0, coarse, lambda c: by_rows(S1, c, coarse, own, spec, 0, near, low))

        def take(c):
            outer_low(c).wait_recv()
            by_rows(S0, c, coarse, outer, spec0, 0, own, full)

            @pl.when(c == 0)
            def _():
                loop(0, held, lambda g: last_on(g).wait_recv())
                by_columns(S2, 0, held, own, spec, 1, far, low)

            @pl.when(c == coarse - 2)
            def _():
                loop(held, groups, lambda g: last_on(g).wait_recv())

            @pl.when(c >= coarse - 2)
            def _():
                loop(
                    jnp.where(c == coarse - 2, 0, c), c + 1,
                    lambda r: by_rows(S3, r, coarse, outer, spec0, 2, far, low),
                )

            loop(jnp.maximum(c - 1, 0), c, delivered(S0, 0))
            loop(0, jnp.where(c == coarse - 1, c, 0), delivered(S3, 1))

        loop(0, coarse, take)
        loop(1, halves, lambda g: by_columns(S2, g, held, own, spec, 1, far, low))
        loop(coarse - 1, coarse, delivered(S0, 0))
        loop(coarse - 1, coarse, delivered(S3, 1))
        loop(0, coarse, lambda c: await_share(S1, c, coarse_rows(c)))

        def ends(slot, sep):
            def body(c):
                where = fine_rows(c)
                give_back(slot, c).wait_recv()
                finish_rows(sep, c, fine, added(slot, where) + back_in[(slot,) + where].astype(f32))

            return body

        loop(0, few, ends(S1, 0))
        loop(0, halves, lambda g: await_share(S2, g, wide_cols(g)))
        loop(0, few, ends(S2, 1))

        def late(c):
            ends(S1, 0)(c)
            ends(S2, 1)(c)

        loop(few, fine, late)
        for copy in own_second():
            copy.wait_send()
        loop(0, fine, lambda c: second_on(own_hbm, c, 2).wait_send())
        loop(0, fine, lambda c: first_on(outer, c, 2).wait_send())
        loop(0, groups, lambda g: third_on(near, g, 0).wait_send())
        for slot in (S0, S1, S3):
            settle(slot, coarse, coarse_rows)
        settle(S2, halves, wide_cols)
        for n in range(2):
            loop(0, coarse, lambda c: deliver(n, c).wait_send())

    @pl.when(freq == 2)
    def _():
        loop(0, groups, lambda g: third_on(own_hbm, g, 1).start())
        clear(1)
        clear(2)
        loading.wait()
        tapers.wait()
        own_second()[0].wait_recv()

        def second(c):
            second_on(own_hbm, c, 2).wait_recv()
            second_on(far, c, 3).start()
            by_rows(S1, c, fine, far, spec1, 0, own, high)

        def first(c):
            first_on(outer, c, 2).wait_recv()
            first_on(near, c, 3).start()

            @pl.when(c < groups)
            def _():
                last_low(c).wait_recv()
                last_on(c).start()

            by_rows(S0, c, fine, near, spec0, 1, own, high)
            loop(0, jnp.where(c == groups, 2, 0), returned(S1))
            before = jnp.where(c == groups, 0, jnp.maximum(c - 1, 0))
            loop(before, jnp.where(c >= groups, c, before), returned(S0))

        def block(g):
            by_columns(S3, g, 1, own, spec, 0, outer, full)

        def block_in(g):
            last_high(g).wait_recv()

        loop(0, 2, second)
        own_first()[1].wait_recv()
        own_second()[2].wait_recv()
        loop(0, fine, first)

        def second_more(c):
            second(c)
            loop(c - 1, jnp.where(c > 2, c, c - 1), returned(S1))
            loop(fine - 1, jnp.where(c == 2, fine, fine - 1), returned(S0))
            g = jnp.where(c < few - 1, c - 2, groups - 2)
            stop = jnp.where(c < 2 + groups - 2, g + 1, jnp.where(c == few - 1, groups - 1, g))
            loop(g, stop, block_in)
            loop(g, stop, block)

        loop(2, few, second_more)
        loop(few - 1, few, returned(S1))

        def tail(c):
            second_on(own_hbm, c, 2).wait_recv()
            by_rows(S1, c, fine, far, spec1, 0, own, high)
            last = jnp.where(c == few, groups, groups - 1)
            loop(groups - 1, last, block_in)
            by_rows(S2, c, fine, far, spec1, 1, outer, high)
            loop(groups - 1, last, block)
            returned(S1)(c)
            returned(S2)(c)

        loop(few, fine, tail)
        for g in range(groups):
            where = cols_of(g)
            await_share(S3, g, where)
            finish(0, 0, rows, g * rows // LANES, added(S3, where))

        loop(0, groups, lambda g: third_on(own_hbm, g, 1).wait_send())
        loop(0, groups, lambda g: last_on(g).wait_send())
        loop(0, fine, lambda c: first_on(near, c, 3).wait_send())
        loop(0, few, lambda c: second_on(far, c, 3).wait_send())
        settle(S0, fine, fine_rows)
        settle(S1, fine, fine_rows)
        settle(S2, fine, fine_rows, few)
        settle(S3, groups, cols_of)
        loop(0, fine, lambda c: give_back(S0, c).wait_send())
        loop(0, fine, lambda c: give_back(S1, c).wait_send())
        loop(few, fine, lambda c: give_back(S2, c).wait_send())

    @pl.when(freq == 3)
    def _():
        loop(0, groups, lambda g: last_low(g).start())
        for sep in range(3):
            clear(sep)
        loading.wait()
        tapers.wait()
        own_second()[1].wait_recv()

        def second(c):
            second_on(far, c, 3).wait_recv()
            by_rows(S2, c, fine, far, spec1, 1, own, high)
            returned(S2)(c)

        def first(c):
            first_on(near, c, 3).wait_recv()
            by_rows(S3, c, fine, near, spec0, 2, own, high)
            returned(S3)(c)
            loop(held, jnp.where(c == fine // 2, groups, held), lambda g: last_high(g).start())

        loop(0, 2, second)
        loop(0, held, lambda g: last_high(g).start())
        own_first()[2].wait_recv()
        loop(0, fine, first)
        loop(2, few, second)
        loop(0, groups, lambda g: last_low(g).wait_send())
        loop(0, groups, lambda g: last_high(g).wait_send())
        settle(S3, fine, fine_rows)
        settle(S2, few, fine_rows)
        loop(0, fine, lambda c: give_back(S3, c).wait_send())
        loop(0, few, lambda c: give_back(S2, c).wait_send())


def meet_covariance(beam_matrix, sky_spectrum, taper_tiles):
    _, parts, modes, width = beam_matrix.shape
    separations, local_rows, _ = taper_tiles.shape
    groups = modes // local_rows
    tiles = 4 * 2 * local_rows * modes
    block = parts * modes * width
    cut = int(width * (0.5 - tiles / (4 * block))) // LANES * LANES
    bf16, f32 = jnp.bfloat16, jnp.float32
    shape = (parts, groups, local_rows, width)
    tile = (2, local_rows, modes)
    blocks = modes // LANES
    dma = pltpu.SemaphoreType.DMA
    pair = lambda *dims: [dma(dims), dma(dims)]
    vmem = pl.BlockSpec(memory_space=pltpu.VMEM)
    hbm = pl.BlockSpec(memory_space=pltpu.HBM)
    spec = jnp.swapaxes(sky_spectrum, 0, 1)
    lines = pl.pallas_call(
        functools.partial(meet_kernel, cut),
        out_shape=jax.ShapeDtypeStruct((separations, local_rows * blocks * 2, LANES), f32),
        in_specs=[hbm, vmem, hbm],
        out_specs=vmem,
        scratch_shapes=[
            pltpu.VMEM(shape, bf16), pltpu.VMEM(taper_tiles.shape, bf16),
            *[pltpu.VMEM(shape, bf16)] * 3,
            *[pltpu.VMEM(spec.shape, f32)] * 2,
            pltpu.VMEM((4, groups) + tile, bf16),
            pltpu.VMEM((4, groups - 1) + tile, bf16),
            *[pltpu.VMEM((4,) + tile, bf16)] * 2,
            *[pltpu.VMEM((2,) + tile, bf16)] * 2,
            dma, dma, *pair(7), *pair(FINE), *pair(max(COARSE, groups)), *pair(groups),
            *pair(FINE), *pair(FINE), *pair(groups),
            *pair(4, FINE, groups - 1), *pair(4, FINE), *pair(2, COARSE),
        ],
        compiler_params=pltpu.CompilerParams(
            collective_id=0, has_side_effects=True, vmem_limit_bytes=51 * 2**20
        ),
    )(beam_matrix[0].reshape(shape), spec, taper_tiles)
    lines = lines.reshape(1, separations, local_rows, blocks, 2, LANES)
    return jnp.swapaxes(lines, 3, 4).reshape(1, separations, local_rows, 2, modes)


def local(beam_matrix, sky_spectrum, taper_tiles, noise_tiles):
    per_device, _, modes, width = beam_matrix.shape
    separations = sky_spectrum.shape[1]
    local_rows = taper_tiles.shape[1]
    in_line = (
        per_device == 1
        and separations == 3
        and lax.axis_size("freq") == separations + 1
        and modes // local_rows == 4
        and local_rows % LANES == 0
        and width % (8 * LANES) == 0
    )
    noise = noise_tiles.astype(jnp.float32)
    if in_line:
        return meet_covariance(beam_matrix, sky_spectrum, taper_tiles) + noise
    summed = general_sums(beam_matrix, sky_spectrum, local_rows)
    summed = summed.reshape(per_device, separations, local_rows, 2, modes)
    taper = taper_tiles.astype(jnp.float32)[None, :, :, None, :]
    return taper * summed + noise


def solution(mesh):
    placed = (
        P(("grp", "freq"), None, None, ("ell", "pol")),
        P(("grp", "freq"), None, ("ell", "pol")),
        P(None, ("ell", "pol"), None),
        P(("grp", "freq"), None, ("ell", "pol"), None, None),
    )
    return jax.shard_map(
        local,
        mesh=mesh,
        in_specs=placed,
        out_specs=P(("grp", "freq"), None, ("ell", "pol"), None, None),
        check_vma=False,
    )
```

```python
import functools

import jax
import jax.numpy as jnp
from jax import lax
from jax.experimental import pallas as pl
from jax.experimental.pallas import tpu as pltpu
from jax.sharding import PartitionSpec as P

FINE = 8
COARSE = 4
LEAD = 2
LATE = 2
EDGE = 2
LANES = 128


def passed_along(block, axis, distance):
    devices = range(lax.axis_size(axis))
    route = [(i - distance, i) for i in devices if i - distance in devices]
    return lax.ppermute(block, axis, route)


def general_sums(beam_matrix, sky_spectrum, local_rows):
    per_device = beam_matrix.shape[0]
    mode_count = beam_matrix.shape[2]
    separations = sky_spectrum.shape[1]
    needed = (per_device - 1 + separations) // per_device
    blocks = [beam_matrix]
    for offset in range(needed):
        blocks.append(passed_along(beam_matrix, "freq", -(offset + 1)))
    term_list = []
    for sep_index in range(separations):
        target = sep_index + 1
        partner = blocks[target // per_device][target % per_device]
        spec_row = sky_spectrum[0, sep_index]
        scaled = (spec_row[None, None, :] * beam_matrix[0].astype(jnp.float32)).astype(jnp.bfloat16)
        right = jnp.concatenate([partner[0], partner[1]], axis=-1)
        top = jnp.concatenate([scaled[0], scaled[1]], axis=-1)
        bottom = jnp.concatenate([scaled[1], -scaled[0]], axis=-1)
        left = jnp.stack([top, bottom], axis=1).reshape(2 * mode_count, top.shape[-1])
        product = lax.dot_general(
            left, right, (((1,), (1,)), ((), ())), preferred_element_type=jnp.float32
        ).reshape(mode_count, 2, mode_count)
        term_list.append(
            lax.psum_scatter(
                product.astype(jnp.bfloat16), ("ell", "pol"), scatter_dimension=0, tiled=True
            ).astype(jnp.float32)
        )
    return jnp.stack(term_list)


S0, S1, S2, S3 = range(4)


def meet_kernel(
    cut, own_hbm, spec_hbm, taper_hbm, out,
    own, spec, taper, outer, near, far, spec0, spec1, stage, inbox, back_out, back_in, final_out, final_in, held_sum,
    load, load_spec, load_taper, spec_s, spec_r, hi_s, hi_r, lo_s, lo_r, mid_s, mid_r, nr_s, nr_r, fr_s, fr_r, fl_s, fl_r,
    rs_s, rs_r, bk_s, bk_r, fn_s, fn_r,
):
    f32, bf16 = jnp.float32, jnp.bfloat16
    _, groups, rows, width = own.shape
    modes = groups * rows
    fine, coarse, halves = FINE, COARSE, 2
    held = groups // halves
    few = fine - LATE
    gap = fine // (groups + 1)
    settled = gap * (groups - 1) + 1
    freqs = lax.axis_size("freq")
    pols = lax.axis_size("pol")
    freq = lax.axis_index("freq")
    me = lax.axis_index("ell") * pols + lax.axis_index("pol")
    low, high, full = (0, cut), (cut, width), (0, width)
    edge = width - EDGE * LANES
    lasts = ((cut, edge), (edge, width))
    every = slice(None)
    per_row = 2 * modes // LANES

    loading = pltpu.make_async_copy(own_hbm, own, load)
    loading.start()
    spectra = pltpu.make_async_copy(spec_hbm, spec, load_spec)
    spectra.start()
    tapers = pltpu.make_async_copy(taper_hbm, taper, load_taper)
    tapers.start()

    barrier = pltpu.get_barrier_semaphore()
    @pl.when(freq > 0)
    def _():
        pl.semaphore_signal(
            barrier, inc=1, device_id={"freq": freq - 1}, device_id_type=pl.DeviceIdType.MESH
        )

    @pl.when(freq < freqs - 1)
    def _():
        pl.semaphore_signal(
            barrier, inc=1, device_id={"freq": freq + 1}, device_id_type=pl.DeviceIdType.MESH
        )

    for d in range(1, groups):
        other = lax.rem(me + d, groups)
        pl.semaphore_signal(
            barrier, inc=1, device_id={"ell": other // pols, "pol": lax.rem(other, pols)},
            device_id_type=pl.DeviceIdType.MESH,
        )
    beside = jnp.where(freq > 0, 1, 0) + jnp.where(freq < freqs - 1, 1, 0)
    pl.semaphore_wait(barrier, beside + groups - 1)

    def span(c, pieces):
        step = rows // pieces
        return pl.ds(pl.multiple_of(c * step, step), step)

    def to_freq(src, dst, send, recv, target):
        return pltpu.make_async_remote_copy(
            src_ref=src, dst_ref=dst, send_sem=send, recv_sem=recv,
            device_id={"freq": target}, device_id_type=pl.DeviceIdType.MESH,
        )

    def lanes(part):
        return pl.ds(part[0], part[1] - part[0])

    def loop(lo, hi, body):
        def wrapped(i, carry):
            body(i)
            return carry

        lax.fori_loop(lo, hi, wrapped, 0)

    def send_spec(src, dst, seps, part, n, target):
        where = (pl.ds(seps[0], len(seps)), every, lanes(part))
        return to_freq(src.at[where], dst.at[where], spec_s.at[n], spec_r.at[n], target)

    def first_rows(target):
        if target == 1:
            return send_spec(spec_hbm, spec0, (0, 1, 2), full, 0, 1)
        return send_spec(spec0, spec0, (1, 2) if target == 2 else (2,), high, target - 1, target)

    def second_rows(target):
        if target == 2:
            return send_spec(spec_hbm, spec1, (0, 1), high, 3, 2)
        return send_spec(spec1, spec1, (1,), high, 4, 3)

    def moved(src, dst, where, send, recv, target):
        return to_freq(src.at[where], dst.at[where], send, recv, target)

    def row_piece(c, pieces, part):
        return (every, every, span(c, pieces), lanes(part))

    def block_piece(g, count, part):
        return (every, pl.ds(g * count, count), every, lanes(part))

    def outer_high(c):
        return moved(own_hbm, outer, row_piece(c, fine, high), hi_s.at[c], hi_r.at[c], 1)

    def outer_low(c):
        return moved(own_hbm, outer, row_piece(c, coarse, low), lo_s.at[c], lo_r.at[c], 1)

    def first_on(src, c, target):
        return moved(src, near, row_piece(c, fine, high), nr_s.at[c], nr_r.at[c], target)

    def second_on(src, c, target):
        return moved(src, far, row_piece(c, fine, high), fr_s.at[c], fr_r.at[c], target)

    def second_last(n):
        where = row_piece(fine - 1, fine, lasts[n])
        m = fine - 1 + n
        return moved(own_hbm, far, where, fr_s.at[m], fr_r.at[m], 2)

    def last_low(g):
        return moved(own_hbm, outer, block_piece(g, 1, low), lo_s.at[g], lo_r.at[g], 2)

    def last_high(g):
        return moved(own_hbm, outer, block_piece(g, 1, high), hi_s.at[g], hi_r.at[g], 2)

    def last_on(g):
        return moved(outer, far, block_piece(g, 1, low), fl_s.at[g], fl_r.at[g], 1)

    def third_on(src, g, target):
        return moved(src, near, block_piece(g, 1, low), mid_s.at[g], mid_r.at[g], target)

    def share(slot, piece, where):
        copies = []
        for d in range(1, groups):
            other = lax.rem(me + d, groups)
            copies.append(
                pltpu.make_async_remote_copy(
                    src_ref=stage.at[(slot, other) + where],
                    dst_ref=inbox.at[(slot, d - 1) + where],
                    send_sem=rs_s.at[slot, piece, d - 1],
                    recv_sem=rs_r.at[slot, piece, d - 1],
                    device_id={"ell": other // pols, "pol": lax.rem(other, pols)},
                    device_id_type=pl.DeviceIdType.MESH,
                )
            )
        return copies

    def start_share(slot, piece, where):
        for copy in share(slot, piece, where):
            copy.start()

    def rows_of(c, pieces):
        return (every, span(c, pieces), every)

    def cols_of(g, count=1):
        size = count * rows
        return (every, every, pl.ds(pl.multiple_of(g * size, size), size))

    def wide_cols(g):
        return cols_of(g, held)

    def dot(a, b):
        return lax.dot_general(a, b, (((1,), (1,)), ((), ())), preferred_element_type=f32)

    def product(left, left_where, weight, right, right_where):
        def scaled(part_index):
            value = left[(part_index,) + left_where].reshape(-1, weight.shape[-1])
            return (weight * value.astype(f32)).astype(bf16)

        a_re, a_im = scaled(0), scaled(1)
        b_re = right[(0,) + right_where].reshape(-1, weight.shape[-1])
        b_im = right[(1,) + right_where].reshape(-1, weight.shape[-1])
        both = dot(jnp.concatenate([a_re, a_im], 0), b_re)
        return both + dot(jnp.concatenate([a_im, -a_re], 0), b_im)

    def cross(*operands):
        both = product(*operands)
        size = both.shape[0] // 2
        return both[:size].astype(bf16), both[size:].astype(bf16)

    def row_operands(c, pieces, left, weights, sep, right, part):
        return (
            left, (every, span(c, pieces), lanes(part)), weights[sep, :, lanes(part)],
            right, (every, every, lanes(part)),
        )

    def by_rows(slot, c, pieces, *rest):
        put_rows(slot, c, pieces, *cross(*row_operands(c, pieces, *rest)))

    def put_rows(slot, c, pieces, real, imag):
        stage[slot, :, 0, span(c, pieces), :] = real.reshape(groups, rows // pieces, modes)
        stage[slot, :, 1, span(c, pieces), :] = imag.reshape(groups, rows // pieces, modes)
        start_share(slot, c, rows_of(c, pieces))

    def by_columns(slot, g, count, left, weights, sep, right, part):
        weight = weights[sep, :, lanes(part)]
        columns = cols_of(g, count)[-1]

        def body(o):
            real, imag = cross(
                left, (o, every, lanes(part)), weight,
                right, (pl.ds(g * count, count), every, lanes(part)),
            )
            stage[slot, o, 0, :, columns] = real
            stage[slot, o, 1, :, columns] = imag

        loop(0, groups, body)
        start_share(slot, g, cols_of(g, count))

    def await_share(slot, piece, where):
        for copy in share(slot, piece, where):
            copy.wait_recv()

    def added(slot, where):
        total = stage[(slot, me) + where].astype(f32)
        for d in range(groups - 1):
            total = total + inbox[(slot, d) + where].astype(f32)
        return total

    def settle(slot, pieces, where_of, lo=0):
        def body(c):
            for copy in share(slot, c, where_of(c)):
                copy.wait_send()

        loop(lo, pieces, body)

    def fine_rows(c):
        return rows_of(c, fine)

    def coarse_rows(c):
        return rows_of(c, coarse)

    def give_back(slot, c):
        where = fine_rows(c)
        return to_freq(
            back_out.at[(slot,) + where], back_in.at[(slot,) + where],
            bk_s.at[slot, c], bk_r.at[slot, c], 0 if slot in (S0, S3) else 1,
        )

    def returned(slot):
        def body(c):
            where = fine_rows(c)
            await_share(slot, c, where)
            back_out[(slot,) + where] = added(slot, where).astype(bf16)
            give_back(slot, c).start()

        return body

    def deliver(n, c):
        where = coarse_rows(c)
        return to_freq(
            final_out.at[(n,) + where], final_in.at[(n,) + where], fn_s.at[n, c], fn_r.at[n, c], 0
        )

    def delivered(slot, n):
        def body(c):
            where = coarse_rows(c)
            await_share(slot, c, where)
            final_out[(n,) + where] = added(slot, where).astype(bf16)
            deliver(n, c).start()

        return body

    def finish(sep, first_row, count, first_block, total):
        weight = taper[sep, pl.ds(first_row, count), pl.ds(first_block * LANES, total.shape[-1])]
        weight = weight.astype(f32)
        for part in range(2):
            value = weight * total[part]
            for j in range(total.shape[-1] // LANES):
                start = first_row * per_row + 2 * (first_block + j) + part
                out[sep, pl.ds(start, count, stride=per_row), :] = value[
                    :, j * LANES:(j + 1) * LANES
                ]

    def finish_rows(sep, c, pieces, total):
        step = rows // pieces
        finish(sep, pl.multiple_of(c * step, step), step, 0, total)

    def clear(sep):
        out[sep] = jnp.zeros(out.shape[1:], f32)

    @pl.when(freq == 0)
    def _():
        outer_high(0).start()
        first_rows(1).start()
        loop(1, fine, lambda c: outer_high(c).start())
        loop(0, coarse, lambda c: outer_low(c).start())
        loading.wait()
        spectra.wait()
        tapers.wait()
        loop(0, groups, lambda g: third_on(near, g, 0).wait_recv())
        loop(0, coarse, lambda c: by_rows(S0, c, coarse, own, spec, 1, near, low))
        loop(0, coarse, lambda c: await_share(S0, c, coarse_rows(c)))

        def ends(c):
            deliver(0, c).wait_recv()
            finish_rows(0, c, coarse, final_in[(0,) + coarse_rows(c)].astype(f32))

        def middles(c):
            where = fine_rows(c)
            give_back(S0, c).wait_recv()
            finish_rows(1, c, fine, added(S0, where) + back_in[(S0,) + where].astype(f32))

        def longs(c):
            per = fine // coarse
            where = fine_rows(c)

            @pl.when(lax.rem(c, per) == 0)
            def _():
                deliver(1, c // per).wait_recv()

            give_back(S3, c).wait_recv()
            total = final_in[(1,) + where].astype(f32) + back_in[(S3,) + where].astype(f32)
            finish_rows(2, c, fine, total)

        loop(0, coarse - 1, ends)
        loop(0, fine, middles)
        loop(coarse - 1, coarse, ends)
        loop(0, fine, longs)
        first_rows(1).wait_send()
        loop(0, fine, lambda c: outer_high(c).wait_send())
        loop(0, coarse, lambda c: outer_low(c).wait_send())
        settle(S0, coarse, coarse_rows)

    @pl.when(freq == 1)
    def _():
        second_on(own_hbm, 0, 2).start()
        second_rows(2).start()
        loop(1, LEAD, lambda c: second_on(own_hbm, c, 2).start())
        first_rows(1).wait_recv()
        first_rows(2).start()
        clear(2)

        def relay(c):
            outer_high(c).wait_recv()
            first_on(outer, c, 2).start()

        def relay_back(g):
            third_on(own_hbm, g, 1).wait_recv()
            third_on(near, g, 0).start()

        done = 0
        for c in range(fine):
            relay(c)
            while done < groups and 2 * fine * (done + 1) <= groups * (2 * c + 3):
                relay_back(done)
                done += 1
        for g in range(done, groups):
            relay_back(g)
        loop(LEAD, fine - 1, lambda c: second_on(own_hbm, c, 2).start())
        for n in range(2):
            second_last(n).start()
        loading.wait()
        spectra.wait()
        tapers.wait()
        loop(0, coarse, lambda c: by_rows(S1, c, coarse, own, spec, 0, near, low))

        def take(c):
            outer_low(c).wait_recv()
            by_rows(S0, c, coarse, outer, spec0, 0, own, full)

            @pl.when(c == 0)
            def _():
                loop(0, held, lambda g: last_on(g).wait_recv())
                by_columns(S2, 0, held, own, spec, 1, far, low)

            @pl.when(c == coarse - 2)
            def _():
                loop(held, groups, lambda g: last_on(g).wait_recv())

            @pl.when(c >= coarse - 2)
            def _():
                loop(
                    jnp.where(c == coarse - 2, 0, c), c + 1,
                    lambda r: by_rows(S3, r, coarse, outer, spec0, 2, far, low),
                )

            loop(jnp.maximum(c - 1, 0), c, delivered(S0, 0))
            loop(0, jnp.where(c == coarse - 1, c, 0), delivered(S3, 1))

        loop(0, coarse, take)
        loop(1, halves, lambda g: by_columns(S2, g, held, own, spec, 1, far, low))
        loop(coarse - 1, coarse, delivered(S0, 0))
        loop(coarse - 1, coarse, delivered(S3, 1))
        loop(0, coarse, lambda c: await_share(S1, c, coarse_rows(c)))

        def ends(slot, sep):
            def body(c):
                where = fine_rows(c)
                give_back(slot, c).wait_recv()
                finish_rows(sep, c, fine, added(slot, where) + back_in[(slot,) + where].astype(f32))

            return body

        loop(0, few, ends(S1, 0))
        loop(0, halves, lambda g: await_share(S2, g, wide_cols(g)))
        loop(0, few, ends(S2, 1))

        def late(c):
            ends(S1, 0)(c)
            ends(S2, 1)(c)

        second_rows(2).wait_send()
        first_rows(2).wait_send()
        loop(0, fine - 1, lambda c: second_on(own_hbm, c, 2).wait_send())
        for n in range(2):
            second_last(n).wait_send()
        loop(0, fine, lambda c: first_on(outer, c, 2).wait_send())
        loop(0, groups, lambda g: third_on(near, g, 0).wait_send())
        for slot in (S0, S1, S3):
            settle(slot, coarse, coarse_rows)
        settle(S2, halves, wide_cols)
        for n in range(2):
            loop(0, coarse, lambda c: deliver(n, c).wait_send())
        loop(few, fine, late)

    @pl.when(freq == 2)
    def _():
        loop(0, groups, lambda g: third_on(own_hbm, g, 1).start())
        clear(1)
        clear(2)
        loading.wait()
        spectra.wait()
        tapers.wait()
        second_rows(2).wait_recv()
        second_rows(3).start()

        def second(c):
            second_on(own_hbm, c, 2).wait_recv()
            second_on(far, c, 3).start()
            by_rows(S1, c, fine, far, spec1, 0, own, high)

        def first(c):
            first_on(outer, c, 2).wait_recv()
            first_on(near, c, 3).start()

            g = c // gap

            @pl.when(jnp.logical_and(lax.rem(c, gap) == 0, g < groups))
            def _():
                last_low(g).wait_recv()
                last_on(g).start()

            by_rows(S0, c, fine, near, spec0, 1, own, high)
            loop(0, jnp.where(c == settled, LEAD, 0), returned(S1))
            before = jnp.where(c == settled, 0, jnp.maximum(c - 1, 0))
            loop(before, jnp.where(c >= settled, c, before), returned(S0))

        def block(g):
            by_columns(S3, g, 1, own, spec, 0, outer, full)

        def block_in(g):
            last_high(g).wait_recv()

        loop(0, LEAD, second)
        first_rows(2).wait_recv()
        first_rows(3).start()
        loop(0, fine, first)

        def second_more(c):
            second(c)
            loop(c - 1, jnp.where(c > LEAD, c, c - 1), returned(S1))
            loop(fine - 1, jnp.where(c == LEAD, fine, fine - 1), returned(S0))
            g = jnp.where(c < LEAD + gap, 0, jnp.where(c < few - gap, 1, 2))
            due = jnp.logical_or(c == LEAD, jnp.logical_or(c == LEAD + gap, c == few - gap))
            loop(g, jnp.where(due, g + 1, g), block_in)
            loop(g, jnp.where(due, g + 1, g), block)

        loop(LEAD, few, second_more)
        loop(few - 1, few, returned(S1))

        def late(c):
            second_on(own_hbm, c, 2).wait_recv()
            by_rows(S1, c, fine, far, spec1, 0, own, high)
            loop(groups - 1, jnp.where(c == few, groups, groups - 1), block_in)
            by_rows(S2, c, fine, far, spec1, 1, outer, high)
            loop(groups - 1, jnp.where(c == few, groups, groups - 1), block)

        loop(few, fine - 1, late)
        c = fine - 1
        ways = ((S1, own), (S2, outer))
        second_last(0).wait_recv()
        for n, (slot, right) in enumerate(ways):
            held_sum[n] = product(*row_operands(c, fine, far, spec1, n, right, lasts[0]))
        loop(few, c, returned(S1))
        loop(few, c, returned(S2))
        second_last(1).wait_recv()
        for n, (slot, right) in enumerate(ways):
            both = held_sum[n] + product(*row_operands(c, fine, far, spec1, n, right, lasts[1]))
            size = both.shape[0] // 2
            put_rows(slot, c, fine, both[:size].astype(bf16), both[size:].astype(bf16))
        returned(S1)(c)
        returned(S2)(c)
        for g in range(groups):
            where = cols_of(g)
            await_share(S3, g, where)
            finish(0, 0, rows, g * rows // LANES, added(S3, where))

        second_rows(3).wait_send()
        first_rows(3).wait_send()
        loop(0, groups, lambda g: third_on(own_hbm, g, 1).wait_send())
        loop(0, groups, lambda g: last_on(g).wait_send())
        loop(0, fine, lambda c: first_on(near, c, 3).wait_send())
        loop(0, few, lambda c: second_on(far, c, 3).wait_send())
        settle(S0, fine, fine_rows)
        settle(S1, fine, fine_rows)
        settle(S2, fine, fine_rows, few)
        settle(S3, groups, cols_of)
        loop(0, fine, lambda c: give_back(S0, c).wait_send())
        loop(0, fine, lambda c: give_back(S1, c).wait_send())
        loop(few, fine, lambda c: give_back(S2, c).wait_send())

    @pl.when(freq == 3)
    def _():
        loop(0, groups, lambda g: last_low(g).start())
        for sep in range(3):
            clear(sep)
        loading.wait()
        spectra.wait()
        tapers.wait()
        second_rows(3).wait_recv()

        def second(c):
            second_on(far, c, 3).wait_recv()
            by_rows(S2, c, fine, far, spec1, 1, own, high)
            returned(S2)(c)

        def first(c):
            first_on(near, c, 3).wait_recv()
            by_rows(S3, c, fine, near, spec0, 2, own, high)
            returned(S3)(c)
            loop(held, jnp.where(c == fine - groups, groups, held), lambda g: last_high(g).start())

        loop(0, LEAD, second)
        loop(0, held, lambda g: last_high(g).start())
        first_rows(3).wait_recv()
        loop(0, fine, first)
        loop(LEAD, few, second)
        loop(0, groups, lambda g: last_low(g).wait_send())
        loop(0, groups, lambda g: last_high(g).wait_send())
        settle(S3, fine, fine_rows)
        settle(S2, few, fine_rows)
        loop(0, fine, lambda c: give_back(S3, c).wait_send())
        loop(0, few, lambda c: give_back(S2, c).wait_send())


def meet_covariance(beam_matrix, sky_spectrum, taper_tiles):
    _, parts, modes, width = beam_matrix.shape
    separations, local_rows, _ = taper_tiles.shape
    groups = modes // local_rows
    tiles = 4 * 2 * local_rows * modes
    block = parts * modes * width
    cut = int(width * (0.5 - tiles / (4 * block))) // LANES * LANES
    bf16, f32 = jnp.bfloat16, jnp.float32
    shape = (parts, groups, local_rows, width)
    tile = (2, local_rows, modes)
    blocks = modes // LANES
    dma = pltpu.SemaphoreType.DMA
    pair = lambda *dims: [dma(dims), dma(dims)]
    vmem = pl.BlockSpec(memory_space=pltpu.VMEM)
    hbm = pl.BlockSpec(memory_space=pltpu.HBM)
    spec = jnp.swapaxes(sky_spectrum, 0, 1)
    kept = lambda array: pltpu.with_memory_space_constraint(array, pltpu.HBM)
    lines = pl.pallas_call(
        functools.partial(meet_kernel, cut),
        out_shape=jax.ShapeDtypeStruct((separations, local_rows * blocks * 2, LANES), f32),
        in_specs=[hbm, hbm, hbm],
        out_specs=vmem,
        scratch_shapes=[
            pltpu.VMEM(shape, bf16), pltpu.VMEM(spec.shape, f32),
            pltpu.VMEM(taper_tiles.shape, bf16),
            *[pltpu.VMEM(shape, bf16)] * 3,
            *[pltpu.VMEM(spec.shape, f32)] * 2,
            pltpu.VMEM((4, groups) + tile, bf16),
            pltpu.VMEM((4, groups - 1) + tile, bf16),
            *[pltpu.VMEM((4,) + tile, bf16)] * 2,
            *[pltpu.VMEM((2,) + tile, bf16)] * 2,
            pltpu.VMEM((2, 2 * modes // FINE, modes), f32),
            dma, dma, dma, *pair(5), *pair(FINE), *pair(max(COARSE, groups)), *pair(groups),
            *pair(FINE), *pair(FINE + 1), *pair(groups),
            *pair(4, FINE, groups - 1), *pair(4, FINE), *pair(2, COARSE),
        ],
        compiler_params=pltpu.CompilerParams(
            collective_id=0, has_side_effects=True, vmem_limit_bytes=51 * 2**20
        ),
    )(kept(beam_matrix[0].reshape(shape)), kept(spec), kept(taper_tiles))
    lines = lines.reshape(1, separations, local_rows, blocks, 2, LANES)
    return jnp.swapaxes(lines, 3, 4).reshape(1, separations, local_rows, 2, modes)


def local(beam_matrix, sky_spectrum, taper_tiles, noise_tiles):
    per_device, _, modes, width = beam_matrix.shape
    separations = sky_spectrum.shape[1]
    local_rows = taper_tiles.shape[1]
    in_line = (
        per_device == 1
        and separations == 3
        and lax.axis_size("freq") == separations + 1
        and modes // local_rows == 4
        and local_rows % LANES == 0
        and width % (8 * LANES) == 0
    )
    noise = noise_tiles.astype(jnp.float32)
    if in_line:
        return meet_covariance(beam_matrix, sky_spectrum, taper_tiles) + noise
    summed = general_sums(beam_matrix, sky_spectrum, local_rows)
    summed = summed.reshape(per_device, separations, local_rows, 2, modes)
    taper = taper_tiles.astype(jnp.float32)[None, :, :, None, :]
    return taper * summed + noise


def solution(mesh):
    placed = (
        P(("grp", "freq"), None, None, ("ell", "pol")),
        P(("grp", "freq"), None, ("ell", "pol")),
        P(None, ("ell", "pol"), None),
        P(("grp", "freq"), None, ("ell", "pol"), None, None),
    )
    return jax.shard_map(
        local,
        mesh=mesh,
        in_specs=placed,
        out_specs=P(("grp", "freq"), None, ("ell", "pol"), None, None),
        check_vma=False,
    )
```

```python
import functools

import jax
import jax.numpy as jnp
from jax import lax
from jax.experimental import pallas as pl
from jax.experimental.pallas import tpu as pltpu
from jax.sharding import PartitionSpec as P

FINE = 8
COARSE = 4
LEAD = 2
LATE = 2
EDGE = 2
LANES = 128


def passed_along(block, axis, distance):
    devices = range(lax.axis_size(axis))
    route = [(i - distance, i) for i in devices if i - distance in devices]
    return lax.ppermute(block, axis, route)


def general_sums(beam_matrix, sky_spectrum, local_rows):
    per_device = beam_matrix.shape[0]
    mode_count = beam_matrix.shape[2]
    separations = sky_spectrum.shape[1]
    needed = (per_device - 1 + separations) // per_device
    blocks = [beam_matrix]
    for offset in range(needed):
        blocks.append(passed_along(beam_matrix, "freq", -(offset + 1)))
    term_list = []
    for sep_index in range(separations):
        target = sep_index + 1
        partner = blocks[target // per_device][target % per_device]
        spec_row = sky_spectrum[0, sep_index]
        scaled = (spec_row[None, None, :] * beam_matrix[0].astype(jnp.float32)).astype(jnp.bfloat16)
        right = jnp.concatenate([partner[0], partner[1]], axis=-1)
        top = jnp.concatenate([scaled[0], scaled[1]], axis=-1)
        bottom = jnp.concatenate([scaled[1], -scaled[0]], axis=-1)
        left = jnp.stack([top, bottom], axis=1).reshape(2 * mode_count, top.shape[-1])
        product = lax.dot_general(
            left, right, (((1,), (1,)), ((), ())), preferred_element_type=jnp.float32
        ).reshape(mode_count, 2, mode_count)
        term_list.append(
            lax.psum_scatter(
                product.astype(jnp.bfloat16), ("ell", "pol"), scatter_dimension=0, tiled=True
            ).astype(jnp.float32)
        )
    return jnp.stack(term_list)


S0, S1, S2, S3 = range(4)


def meet_kernel(
    cut, own_hbm, spec_hbm, taper_hbm, out,
    own, spec, taper, outer, near, far, spec0, spec1, stage, inbox, back_out, back_in, final_out, final_in, held_sum, base, pair_out, pair_in,
    load, load_spec, load_taper, spec_s, spec_r, hi_s, hi_r, lo_s, lo_r, mid_s, mid_r, nr_s, nr_r, fr_s, fr_r, fl_s, fl_r,
    rs_s, rs_r, bk_s, bk_r, fn_s, fn_r, pair_s, pair_r,
):
    f32, bf16 = jnp.float32, jnp.bfloat16
    _, groups, rows, width = own.shape
    modes = groups * rows
    fine, coarse, halves = FINE, COARSE, 2
    held = groups // halves
    few = fine - LATE
    gap = fine // (groups + 1)
    settled = gap * (groups - 1) + 1
    freqs = lax.axis_size("freq")
    pols = lax.axis_size("pol")
    freq = lax.axis_index("freq")
    line, core = lax.axis_index("ell"), lax.axis_index("pol")
    me = line * pols + core
    low, high, full = (0, cut), (cut, width), (0, width)
    edge = width - EDGE * LANES
    lasts = ((cut, edge), (edge, width))
    every = slice(None)
    per_row = 2 * modes // LANES

    loading = pltpu.make_async_copy(own_hbm, own, load)
    loading.start()
    spectra = pltpu.make_async_copy(spec_hbm, spec, load_spec)
    spectra.start()
    tapers = pltpu.make_async_copy(taper_hbm, taper, load_taper)
    tapers.start()

    barrier = pltpu.get_barrier_semaphore()
    @pl.when(freq > 0)
    def _():
        pl.semaphore_signal(
            barrier, inc=1, device_id={"freq": freq - 1}, device_id_type=pl.DeviceIdType.MESH
        )

    @pl.when(freq < freqs - 1)
    def _():
        pl.semaphore_signal(
            barrier, inc=1, device_id={"freq": freq + 1}, device_id_type=pl.DeviceIdType.MESH
        )

    for d in range(1, groups):
        other = lax.rem(me + d, groups)
        pl.semaphore_signal(
            barrier, inc=1, device_id={"ell": other // pols, "pol": lax.rem(other, pols)},
            device_id_type=pl.DeviceIdType.MESH,
        )
    beside = jnp.where(freq > 0, 1, 0) + jnp.where(freq < freqs - 1, 1, 0)
    pl.semaphore_wait(barrier, beside + groups - 1)

    def span(c, pieces):
        step = rows // pieces
        return pl.ds(pl.multiple_of(c * step, step), step)

    def to_freq(src, dst, send, recv, target):
        return pltpu.make_async_remote_copy(
            src_ref=src, dst_ref=dst, send_sem=send, recv_sem=recv,
            device_id={"freq": target}, device_id_type=pl.DeviceIdType.MESH,
        )

    def lanes(part):
        return pl.ds(part[0], part[1] - part[0])

    def loop(lo, hi, body):
        def wrapped(i, carry):
            body(i)
            return carry

        lax.fori_loop(lo, hi, wrapped, 0)

    def send_spec(src, dst, seps, part, n, target):
        where = (pl.ds(seps[0], len(seps)), every, lanes(part))
        return to_freq(src.at[where], dst.at[where], spec_s.at[n], spec_r.at[n], target)

    def first_rows(target):
        if target == 1:
            return send_spec(spec_hbm, spec0, (0, 1, 2), full, 0, 1)
        return send_spec(spec0, spec0, (1, 2) if target == 2 else (2,), high, target - 1, target)

    def second_rows(target):
        if target == 2:
            return send_spec(spec_hbm, spec1, (0, 1), high, 3, 2)
        return send_spec(spec1, spec1, (1,), high, 4, 3)

    def moved(src, dst, where, send, recv, target):
        return to_freq(src.at[where], dst.at[where], send, recv, target)

    def row_piece(c, pieces, part):
        return (every, every, span(c, pieces), lanes(part))

    def block_piece(g, count, part):
        return (every, pl.ds(g * count, count), every, lanes(part))

    def outer_high(c):
        return moved(own_hbm, outer, row_piece(c, fine, high), hi_s.at[c], hi_r.at[c], 1)

    def outer_low(c):
        return moved(own_hbm, outer, row_piece(c, coarse, low), lo_s.at[c], lo_r.at[c], 1)

    def first_on(src, c, target):
        return moved(src, near, row_piece(c, fine, high), nr_s.at[c], nr_r.at[c], target)

    def second_on(src, c, target):
        return moved(src, far, row_piece(c, fine, high), fr_s.at[c], fr_r.at[c], target)

    def second_last(n):
        where = row_piece(fine - 1, fine, lasts[n])
        m = fine - 1 + n
        return moved(own_hbm, far, where, fr_s.at[m], fr_r.at[m], 2)

    def last_low(g):
        return moved(own_hbm, outer, block_piece(g, 1, low), lo_s.at[g], lo_r.at[g], 2)

    def last_high(g):
        return moved(own_hbm, outer, block_piece(g, 1, high), hi_s.at[g], hi_r.at[g], 2)

    def last_on(g):
        return moved(outer, far, block_piece(g, 1, low), fl_s.at[g], fl_r.at[g], 1)

    def third_on(src, g, target):
        return moved(src, near, block_piece(g, 1, low), mid_s.at[g], mid_r.at[g], target)

    def share(slot, piece, where):
        copies = []
        for d in range(1, groups):
            other = lax.rem(me + d, groups)
            copies.append(
                pltpu.make_async_remote_copy(
                    src_ref=stage.at[(slot, other) + where],
                    dst_ref=inbox.at[(slot, d - 1) + where],
                    send_sem=rs_s.at[slot, piece, d - 1],
                    recv_sem=rs_r.at[slot, piece, d - 1],
                    device_id={"ell": other // pols, "pol": lax.rem(other, pols)},
                    device_id_type=pl.DeviceIdType.MESH,
                )
            )
        return copies

    def start_share(slot, piece, where):
        for copy in share(slot, piece, where):
            copy.start()

    def rows_of(c, pieces):
        return (every, span(c, pieces), every)

    def cols_of(g, count=1):
        size = count * rows
        return (every, every, pl.ds(pl.multiple_of(g * size, size), size))

    def wide_cols(g):
        return cols_of(g, held)

    def dot(a, b):
        return lax.dot_general(a, b, (((1,), (1,)), ((), ())), preferred_element_type=f32)

    def product(left, left_where, weight, right, right_where):
        def scaled(part_index):
            value = left[(part_index,) + left_where].reshape(-1, weight.shape[-1])
            return (weight * value.astype(f32)).astype(bf16)

        a_re, a_im = scaled(0), scaled(1)
        b_re = right[(0,) + right_where].reshape(-1, weight.shape[-1])
        b_im = right[(1,) + right_where].reshape(-1, weight.shape[-1])
        both = dot(jnp.concatenate([a_re, a_im], 0), b_re)
        return both + dot(jnp.concatenate([a_im, -a_re], 0), b_im)

    def cross(*operands):
        both = product(*operands)
        size = both.shape[0] // 2
        return both[:size].astype(bf16), both[size:].astype(bf16)

    def row_operands(c, pieces, left, weights, sep, right, part):
        return (
            left, (every, span(c, pieces), lanes(part)), weights[sep, :, lanes(part)],
            right, (every, every, lanes(part)),
        )

    def by_rows(slot, c, pieces, *rest):
        put_rows(slot, c, pieces, *cross(*row_operands(c, pieces, *rest)))
        start_share(slot, c, rows_of(c, pieces))

    def put_rows(slot, c, pieces, real, imag):
        stage[slot, :, 0, span(c, pieces), :] = real.reshape(groups, rows // pieces, modes)
        stage[slot, :, 1, span(c, pieces), :] = imag.reshape(groups, rows // pieces, modes)

    def column_product(o, g, count, left, weights, sep, right, part):
        return product(
            left, (pl.ds(o * held, held), every, lanes(part)), weights[sep, :, lanes(part)],
            right, (pl.ds(g * count, count), every, lanes(part)),
        )

    def by_columns(slot, g, count, *operands, base=None):
        columns = cols_of(g, count)[-1]

        def body(o):
            both = column_product(o, g, count, *operands)
            both = both if base is None else both + base[o]
            size = both.shape[0] // 2
            real, imag = both[:size].astype(bf16), both[size:].astype(bf16)
            stage[slot, pl.ds(o * held, held), 0, :, columns] = real.reshape(held, rows, -1)
            stage[slot, pl.ds(o * held, held), 1, :, columns] = imag.reshape(held, rows, -1)

        loop(0, halves, body)
        start_share(slot, g, cols_of(g, count))

    def await_share(slot, piece, where):
        for copy in share(slot, piece, where):
            copy.wait_recv()

    def added(slot, where):
        total = stage[(slot, me) + where].astype(f32)
        for d in range(groups - 1):
            total = total + inbox[(slot, d) + where].astype(f32)
        return total

    def settle(slot, pieces, where_of, lo=0):
        def body(c):
            for copy in share(slot, c, where_of(c)):
                copy.wait_send()

        loop(lo, pieces, body)

    def fine_rows(c):
        return rows_of(c, fine)

    def coarse_rows(c):
        return rows_of(c, coarse)

    def give_back(slot, c):
        where = fine_rows(c)
        return to_freq(
            back_out.at[(slot,) + where], back_in.at[(slot,) + where],
            bk_s.at[slot, c], bk_r.at[slot, c], 0 if slot in (S0, S3) else 1,
        )

    def returned(slot):
        def body(c):
            where = fine_rows(c)
            await_share(slot, c, where)
            back_out[(slot,) + where] = added(slot, where).astype(bf16)
            give_back(slot, c).start()

        return body

    def paired(slot):
        where = fine_rows(fine - 1)
        return [
            pltpu.make_async_remote_copy(
                src_ref=stage.at[(slot, e * pols + 1 - core) + where],
                dst_ref=inbox.at[(slot, e) + where],
                send_sem=rs_s.at[slot, fine - 1, e], recv_sem=rs_r.at[slot, fine - 1, e],
                device_id={"pol": 1 - core}, device_id_type=pl.DeviceIdType.MESH,
            )
            for e in range(groups // pols)
        ]

    def pair_on(n, e, origin):
        return pltpu.make_async_remote_copy(
            src_ref=pair_out.at[n, e], dst_ref=pair_in.at[n, origin],
            send_sem=pair_s.at[n, e], recv_sem=pair_r.at[n, origin],
            device_id={"freq": 1, "ell": e}, device_id_type=pl.DeviceIdType.MESH,
        )

    def pairs_sent(n, slot):
        where = fine_rows(fine - 1)
        for copy in paired(slot):
            copy.wait_recv()
        for e in range(groups // pols):
            total = stage[(slot, e * pols + core) + where].astype(f32)
            total = total + inbox[(slot, e) + where].astype(f32)
            pair_out[n, e] = total.astype(bf16)
        pair_on(n, 1 - line, line).start()
        pair_on(n, line, line).start()

    def deliver(n, c):
        where = coarse_rows(c)
        return to_freq(
            final_out.at[(n,) + where], final_in.at[(n,) + where], fn_s.at[n, c], fn_r.at[n, c], 0
        )

    def delivered(slot, n):
        def body(c):
            where = coarse_rows(c)
            await_share(slot, c, where)
            final_out[(n,) + where] = added(slot, where).astype(bf16)
            deliver(n, c).start()

        return body

    def finish(sep, first_row, count, first_block, total):
        weight = taper[sep, pl.ds(first_row, count), pl.ds(first_block * LANES, total.shape[-1])]
        weight = weight.astype(f32)
        for part in range(2):
            value = weight * total[part]
            for j in range(total.shape[-1] // LANES):
                start = first_row * per_row + 2 * (first_block + j) + part
                out[sep, pl.ds(start, count, stride=per_row), :] = value[
                    :, j * LANES:(j + 1) * LANES
                ]

    def finish_rows(sep, c, pieces, total):
        step = rows // pieces
        finish(sep, pl.multiple_of(c * step, step), step, 0, total)

    def clear(sep):
        out[sep] = jnp.zeros(out.shape[1:], f32)

    @pl.when(freq == 0)
    def _():
        outer_high(0).start()
        first_rows(1).start()
        loop(1, fine, lambda c: outer_high(c).start())
        loop(0, coarse, lambda c: outer_low(c).start())
        loading.wait()
        spectra.wait()
        tapers.wait()
        loop(0, groups, lambda g: third_on(near, g, 0).wait_recv())
        loop(0, coarse, lambda c: by_rows(S0, c, coarse, own, spec, 1, near, low))
        loop(0, coarse, lambda c: await_share(S0, c, coarse_rows(c)))

        def ends(c):
            deliver(0, c).wait_recv()
            finish_rows(0, c, coarse, final_in[(0,) + coarse_rows(c)].astype(f32))

        def middles(c):
            where = fine_rows(c)
            give_back(S0, c).wait_recv()
            finish_rows(1, c, fine, added(S0, where) + back_in[(S0,) + where].astype(f32))

        def longs(c):
            per = fine // coarse
            where = fine_rows(c)

            @pl.when(lax.rem(c, per) == 0)
            def _():
                deliver(1, c // per).wait_recv()

            give_back(S3, c).wait_recv()
            total = final_in[(1,) + where].astype(f32) + back_in[(S3,) + where].astype(f32)
            finish_rows(2, c, fine, total)

        loop(0, coarse - 1, ends)
        loop(0, fine, middles)
        loop(coarse - 1, coarse, ends)
        loop(0, fine, longs)
        first_rows(1).wait_send()
        loop(0, fine, lambda c: outer_high(c).wait_send())
        loop(0, coarse, lambda c: outer_low(c).wait_send())
        settle(S0, coarse, coarse_rows)

    @pl.when(freq == 1)
    def _():
        second_on(own_hbm, 0, 2).start()
        second_rows(2).start()
        loop(1, LEAD, lambda c: second_on(own_hbm, c, 2).start())
        first_rows(1).wait_recv()
        first_rows(2).start()
        clear(2)

        def relay(c):
            outer_high(c).wait_recv()
            first_on(outer, c, 2).start()

        def relay_back(g):
            third_on(own_hbm, g, 1).wait_recv()
            third_on(near, g, 0).start()

        done = 0
        for c in range(fine):
            relay(c)
            while done < groups and 2 * fine * (done + 1) <= groups * (2 * c + 3):
                relay_back(done)
                done += 1
        for g in range(done, groups):
            relay_back(g)
        loop(LEAD, fine - 1, lambda c: second_on(own_hbm, c, 2).start())
        for n in range(2):
            second_last(n).start()
        loading.wait()
        spectra.wait()
        tapers.wait()
        loop(0, coarse, lambda c: by_rows(S1, c, coarse, own, spec, 0, near, low))

        def take(c):
            outer_low(c).wait_recv()
            by_rows(S0, c, coarse, outer, spec0, 0, own, full)

            @pl.when(c == 0)
            def _():
                loop(0, held, lambda g: last_on(g).wait_recv())
                by_columns(S2, 0, held, own, spec, 1, far, low)

            @pl.when(c == coarse - 2)
            def _():
                loop(held, groups, lambda g: last_on(g).wait_recv())

            @pl.when(c >= coarse - 2)
            def _():
                loop(
                    jnp.where(c == coarse - 2, 0, c), c + 1,
                    lambda r: by_rows(S3, r, coarse, outer, spec0, 2, far, low),
                )

            loop(jnp.maximum(c - 1, 0), c, delivered(S0, 0))
            loop(0, jnp.where(c == coarse - 1, c, 0), delivered(S3, 1))

        loop(0, coarse, take)
        loop(1, halves, lambda g: by_columns(S2, g, held, own, spec, 1, far, low))
        loop(coarse - 1, coarse, delivered(S0, 0))
        loop(coarse - 1, coarse, delivered(S3, 1))
        loop(0, coarse, lambda c: await_share(S1, c, coarse_rows(c)))

        def ends(slot, sep):
            def body(c):
                where = fine_rows(c)
                give_back(slot, c).wait_recv()
                finish_rows(sep, c, fine, added(slot, where) + back_in[(slot,) + where].astype(f32))

            return body

        loop(0, few, ends(S1, 0))
        loop(0, halves, lambda g: await_share(S2, g, wide_cols(g)))
        loop(0, few, ends(S2, 1))

        def late(c):
            ends(S1, 0)(c)
            ends(S2, 1)(c)

        second_rows(2).wait_send()
        first_rows(2).wait_send()
        loop(0, fine - 1, lambda c: second_on(own_hbm, c, 2).wait_send())
        for n in range(2):
            second_last(n).wait_send()
        loop(0, fine, lambda c: first_on(outer, c, 2).wait_send())
        loop(0, groups, lambda g: third_on(near, g, 0).wait_send())
        for slot in (S0, S1, S3):
            settle(slot, coarse, coarse_rows)
        settle(S2, halves, wide_cols)
        for n in range(2):
            loop(0, coarse, lambda c: deliver(n, c).wait_send())
        loop(few, fine - 1, late)
        where = fine_rows(fine - 1)
        for n, slot in enumerate((S1, S2)):
            total = added(slot, where)
            for e in range(groups // pols):
                pair_on(n, line, e).wait_recv()
                total = total + pair_in[n, e].astype(f32)
            finish_rows(n, fine - 1, fine, total)

    @pl.when(freq == 2)
    def _():
        loop(0, groups, lambda g: third_on(own_hbm, g, 1).start())
        clear(1)
        clear(2)
        loading.wait()
        spectra.wait()
        tapers.wait()
        second_rows(2).wait_recv()
        second_rows(3).start()

        def second(c):
            second_on(own_hbm, c, 2).wait_recv()
            second_on(far, c, 3).start()
            by_rows(S1, c, fine, far, spec1, 0, own, high)

        def first(c):
            first_on(outer, c, 2).wait_recv()
            first_on(near, c, 3).start()

            g = c // gap

            @pl.when(jnp.logical_and(lax.rem(c, gap) == 0, g < groups))
            def _():
                last_low(g).wait_recv()
                last_on(g).start()

            by_rows(S0, c, fine, near, spec0, 1, own, high)
            loop(0, jnp.where(c == settled, LEAD, 0), returned(S1))
            before = jnp.where(c == settled, 0, jnp.maximum(c - 1, 0))
            loop(before, jnp.where(c >= settled, c, before), returned(S0))

        def block(g):
            by_columns(S3, g, 1, own, spec, 0, outer, full)

        def block_in(g):
            last_high(g).wait_recv()

        def last_base(o):
            base[o] = column_product(o, groups - 1, 1, own, spec, 0, outer, low)

        def last_block(g):
            by_columns(S3, g, 1, own, spec, 0, outer, high, base=base)

        loop(0, LEAD, second)
        first_rows(2).wait_recv()
        first_rows(3).start()
        loop(0, fine, first)

        def second_more(c):
            second(c)
            loop(c - 1, jnp.where(c > LEAD, c, c - 1), returned(S1))
            loop(fine - 1, jnp.where(c == LEAD, fine, fine - 1), returned(S0))
            g = jnp.where(c < LEAD + gap, 0, jnp.where(c < few - gap, 1, 2))
            due = jnp.logical_or(c == LEAD, jnp.logical_or(c == LEAD + gap, c == few - gap))
            loop(g, jnp.where(due, g + 1, g), block_in)
            loop(g, jnp.where(due, g + 1, g), block)

        loop(0, halves, last_base)
        loop(LEAD, few, second_more)
        loop(few - 1, few, returned(S1))

        def late(c):
            second_on(own_hbm, c, 2).wait_recv()
            by_rows(S1, c, fine, far, spec1, 0, own, high)
            loop(groups - 1, jnp.where(c == few, groups, groups - 1), block_in)
            by_rows(S2, c, fine, far, spec1, 1, outer, high)
            loop(groups - 1, jnp.where(c == few, groups, groups - 1), last_block)

        loop(few, fine - 1, late)
        c = fine - 1
        ways = ((S1, own), (S2, outer))
        second_last(0).wait_recv()
        for n, (slot, right) in enumerate(ways):
            held_sum[n] = product(*row_operands(c, fine, far, spec1, n, right, lasts[0]))
        loop(few, c, returned(S1))
        loop(few, c, returned(S2))
        second_last(1).wait_recv()
        for n, (slot, right) in enumerate(ways):
            both = held_sum[n] + product(*row_operands(c, fine, far, spec1, n, right, lasts[1]))
            size = both.shape[0] // 2
            put_rows(slot, c, fine, both[:size].astype(bf16), both[size:].astype(bf16))
            for copy in paired(slot):
                copy.start()
        pairs_sent(0, S1)
        pairs_sent(1, S2)
        for g in range(groups):
            where = cols_of(g)
            await_share(S3, g, where)
            finish(0, 0, rows, g * rows // LANES, added(S3, where))

        second_rows(3).wait_send()
        first_rows(3).wait_send()
        loop(0, groups, lambda g: third_on(own_hbm, g, 1).wait_send())
        loop(0, groups, lambda g: last_on(g).wait_send())
        loop(0, fine, lambda c: first_on(near, c, 3).wait_send())
        loop(0, few, lambda c: second_on(far, c, 3).wait_send())
        settle(S0, fine, fine_rows)
        settle(S1, fine - 1, fine_rows)
        settle(S2, fine - 1, fine_rows, few)
        for n, slot in enumerate((S1, S2)):
            for copy in paired(slot):
                copy.wait_send()
            for e in range(groups // pols):
                pair_on(n, e, line).wait_send()
        settle(S3, groups, cols_of)
        loop(0, fine, lambda c: give_back(S0, c).wait_send())
        loop(0, fine - 1, lambda c: give_back(S1, c).wait_send())
        loop(few, fine - 1, lambda c: give_back(S2, c).wait_send())

    @pl.when(freq == 3)
    def _():
        loop(0, groups, lambda g: last_low(g).start())
        for sep in range(3):
            clear(sep)
        loading.wait()
        spectra.wait()
        tapers.wait()
        second_rows(3).wait_recv()

        def second(c):
            second_on(far, c, 3).wait_recv()
            by_rows(S2, c, fine, far, spec1, 1, own, high)
            returned(S2)(c)

        def first(c):
            first_on(near, c, 3).wait_recv()
            by_rows(S3, c, fine, near, spec0, 2, own, high)
            returned(S3)(c)
            loop(held, jnp.where(c == fine - groups, groups, held), lambda g: last_high(g).start())

        loop(0, LEAD, second)
        loop(0, held, lambda g: last_high(g).start())
        first_rows(3).wait_recv()
        loop(0, fine, first)
        loop(LEAD, few, second)
        loop(0, groups, lambda g: last_low(g).wait_send())
        loop(0, groups, lambda g: last_high(g).wait_send())
        settle(S3, fine, fine_rows)
        settle(S2, few, fine_rows)
        loop(0, fine, lambda c: give_back(S3, c).wait_send())
        loop(0, few, lambda c: give_back(S2, c).wait_send())


def meet_covariance(beam_matrix, sky_spectrum, taper_tiles):
    _, parts, modes, width = beam_matrix.shape
    separations, local_rows, _ = taper_tiles.shape
    groups = modes // local_rows
    tiles = 4 * 2 * local_rows * modes
    block = parts * modes * width
    cut = int(width * (0.5 - tiles / (4 * block))) // LANES * LANES
    bf16, f32 = jnp.bfloat16, jnp.float32
    shape = (parts, groups, local_rows, width)
    tile = (2, local_rows, modes)
    blocks = modes // LANES
    dma = pltpu.SemaphoreType.DMA
    pair = lambda *dims: [dma(dims), dma(dims)]
    vmem = pl.BlockSpec(memory_space=pltpu.VMEM)
    hbm = pl.BlockSpec(memory_space=pltpu.HBM)
    spec = jnp.swapaxes(sky_spectrum, 0, 1)
    kept = lambda array: pltpu.with_memory_space_constraint(array, pltpu.HBM)
    lines = pl.pallas_call(
        functools.partial(meet_kernel, cut),
        out_shape=jax.ShapeDtypeStruct((separations, local_rows * blocks * 2, LANES), f32),
        in_specs=[hbm, hbm, hbm],
        out_specs=vmem,
        scratch_shapes=[
            pltpu.VMEM(shape, bf16), pltpu.VMEM(spec.shape, f32),
            pltpu.VMEM(taper_tiles.shape, bf16),
            *[pltpu.VMEM(shape, bf16)] * 3,
            *[pltpu.VMEM(spec.shape, f32)] * 2,
            pltpu.VMEM((4, groups) + tile, bf16),
            pltpu.VMEM((4, groups - 1) + tile, bf16),
            *[pltpu.VMEM((4,) + tile, bf16)] * 2,
            *[pltpu.VMEM((2,) + tile, bf16)] * 2,
            pltpu.VMEM((2, 2 * modes // FINE, modes), f32),
            pltpu.VMEM((2, modes, local_rows), f32),
            *[pltpu.VMEM((2, 2, 2, local_rows // FINE, modes), bf16)] * 2,
            dma, dma, dma, *pair(5), *pair(FINE), *pair(max(COARSE, groups)), *pair(groups),
            *pair(FINE), *pair(FINE + 1), *pair(groups),
            *pair(4, FINE, groups - 1), *pair(4, FINE), *pair(2, COARSE), *pair(2, 2),
        ],
        compiler_params=pltpu.CompilerParams(
            collective_id=0, has_side_effects=True, vmem_limit_bytes=51 * 2**20
        ),
    )(kept(beam_matrix[0].reshape(shape)), kept(spec), kept(taper_tiles))
    lines = lines.reshape(1, separations, local_rows, blocks, 2, LANES)
    return jnp.swapaxes(lines, 3, 4).reshape(1, separations, local_rows, 2, modes)


def local(beam_matrix, sky_spectrum, taper_tiles, noise_tiles):
    per_device, _, modes, width = beam_matrix.shape
    separations = sky_spectrum.shape[1]
    local_rows = taper_tiles.shape[1]
    in_line = (
        per_device == 1
        and separations == 3
        and lax.axis_size("freq") == separations + 1
        and modes // local_rows == 4
        and lax.axis_size("pol") == 2
        and local_rows % LANES == 0
        and width % (8 * LANES) == 0
    )
    noise = noise_tiles.astype(jnp.float32)
    if in_line:
        return meet_covariance(beam_matrix, sky_spectrum, taper_tiles) + noise
    summed = general_sums(beam_matrix, sky_spectrum, local_rows)
    summed = summed.reshape(per_device, separations, local_rows, 2, modes)
    taper = taper_tiles.astype(jnp.float32)[None, :, :, None, :]
    return taper * summed + noise


def solution(mesh):
    placed = (
        P(("grp", "freq"), None, None, ("ell", "pol")),
        P(("grp", "freq"), None, ("ell", "pol")),
        P(None, ("ell", "pol"), None),
        P(("grp", "freq"), None, ("ell", "pol"), None, None),
    )
    return jax.shard_map(
        local,
        mesh=mesh,
        in_specs=placed,
        out_specs=P(("grp", "freq"), None, ("ell", "pol"), None, None),
        check_vma=False,
    )
```

```python
import functools

import jax
import jax.numpy as jnp
from jax import lax
from jax.experimental import pallas as pl
from jax.experimental.pallas import tpu as pltpu
from jax.sharding import PartitionSpec as P

FINE = 8
COARSE = 4
LEAD = 2
LATE = 2
EDGE = 2
LANES = 128


def passed_along(block, axis, distance):
    devices = range(lax.axis_size(axis))
    route = [(i - distance, i) for i in devices if i - distance in devices]
    return lax.ppermute(block, axis, route)


def general_sums(beam_matrix, sky_spectrum, local_rows):
    per_device = beam_matrix.shape[0]
    mode_count = beam_matrix.shape[2]
    separations = sky_spectrum.shape[1]
    needed = (per_device - 1 + separations) // per_device
    blocks = [beam_matrix]
    for offset in range(needed):
        blocks.append(passed_along(beam_matrix, "freq", -(offset + 1)))
    term_list = []
    for sep_index in range(separations):
        target = sep_index + 1
        partner = blocks[target // per_device][target % per_device]
        spec_row = sky_spectrum[0, sep_index]
        scaled = (spec_row[None, None, :] * beam_matrix[0].astype(jnp.float32)).astype(jnp.bfloat16)
        right = jnp.concatenate([partner[0], partner[1]], axis=-1)
        top = jnp.concatenate([scaled[0], scaled[1]], axis=-1)
        bottom = jnp.concatenate([scaled[1], -scaled[0]], axis=-1)
        left = jnp.stack([top, bottom], axis=1).reshape(2 * mode_count, top.shape[-1])
        product = lax.dot_general(
            left, right, (((1,), (1,)), ((), ())), preferred_element_type=jnp.float32
        ).reshape(mode_count, 2, mode_count)
        term_list.append(
            lax.psum_scatter(
                product.astype(jnp.bfloat16), ("ell", "pol"), scatter_dimension=0, tiled=True
            ).astype(jnp.float32)
        )
    return jnp.stack(term_list)


S0, S1, S2, S3 = range(4)


def meet_kernel(
    cut, own_hbm, spec_hbm, taper_hbm, noise_hbm, out,
    own, spec, taper, noise, outer, near, far, spec0, spec1, stage, inbox, back_out, back_in, final_out, final_in, held_sum, base, pair_out, pair_in,
    load, load_spec, load_taper, load_noise, spec_s, spec_r, hi_s, hi_r, lo_s, lo_r, mid_s, mid_r, nr_s, nr_r, fr_s, fr_r, fl_s, fl_r,
    rs_s, rs_r, bk_s, bk_r, fn_s, fn_r, pair_s, pair_r,
):
    f32, bf16 = jnp.float32, jnp.bfloat16
    _, groups, rows, width = own.shape
    modes = groups * rows
    fine, coarse, halves = FINE, COARSE, 2
    held = groups // halves
    few = fine - LATE
    gap = fine // (groups + 1)
    settled = gap * (groups - 1) + 1
    freqs = lax.axis_size("freq")
    pols = lax.axis_size("pol")
    freq = lax.axis_index("freq")
    line, core = lax.axis_index("ell"), lax.axis_index("pol")
    me = line * pols + core
    low, high, full = (0, cut), (cut, width), (0, width)
    edge = width - EDGE * LANES
    lasts = ((cut, edge), (edge, width))
    every = slice(None)
    per_row = 2 * modes // LANES

    loading = pltpu.make_async_copy(own_hbm, own, load)
    loading.start()
    spectra = pltpu.make_async_copy(spec_hbm, spec, load_spec)
    spectra.start()
    tapers = pltpu.make_async_copy(taper_hbm, taper, load_taper)
    tapers.start()
    noises = pltpu.make_async_copy(noise_hbm, noise, load_noise)
    noises.start()

    barrier = pltpu.get_barrier_semaphore()
    @pl.when(freq > 0)
    def _():
        pl.semaphore_signal(
            barrier, inc=1, device_id={"freq": freq - 1}, device_id_type=pl.DeviceIdType.MESH
        )

    @pl.when(freq < freqs - 1)
    def _():
        pl.semaphore_signal(
            barrier, inc=1, device_id={"freq": freq + 1}, device_id_type=pl.DeviceIdType.MESH
        )

    for d in range(1, groups):
        other = lax.rem(me + d, groups)
        pl.semaphore_signal(
            barrier, inc=1, device_id={"ell": other // pols, "pol": lax.rem(other, pols)},
            device_id_type=pl.DeviceIdType.MESH,
        )
    beside = jnp.where(freq > 0, 1, 0) + jnp.where(freq < freqs - 1, 1, 0)
    pl.semaphore_wait(barrier, beside + groups - 1)

    def span(c, pieces):
        step = rows // pieces
        return pl.ds(pl.multiple_of(c * step, step), step)

    def to_freq(src, dst, send, recv, target):
        return pltpu.make_async_remote_copy(
            src_ref=src, dst_ref=dst, send_sem=send, recv_sem=recv,
            device_id={"freq": target}, device_id_type=pl.DeviceIdType.MESH,
        )

    def lanes(part):
        return pl.ds(part[0], part[1] - part[0])

    def loop(lo, hi, body):
        def wrapped(i, carry):
            body(i)
            return carry

        lax.fori_loop(lo, hi, wrapped, 0)

    def send_spec(src, dst, seps, part, n, target):
        where = (pl.ds(seps[0], len(seps)), every, lanes(part))
        return to_freq(src.at[where], dst.at[where], spec_s.at[n], spec_r.at[n], target)

    def first_rows(target):
        if target == 1:
            return send_spec(spec_hbm, spec0, (0, 1, 2), full, 0, 1)
        return send_spec(spec0, spec0, (1, 2) if target == 2 else (2,), high, target - 1, target)

    def second_rows(target):
        if target == 2:
            return send_spec(spec_hbm, spec1, (0, 1), high, 3, 2)
        return send_spec(spec1, spec1, (1,), high, 4, 3)

    def moved(src, dst, where, send, recv, target):
        return to_freq(src.at[where], dst.at[where], send, recv, target)

    def row_piece(c, pieces, part):
        return (every, every, span(c, pieces), lanes(part))

    def block_piece(g, count, part):
        return (every, pl.ds(g * count, count), every, lanes(part))

    def outer_high(c):
        return moved(own_hbm, outer, row_piece(c, fine, high), hi_s.at[c], hi_r.at[c], 1)

    def outer_low(c):
        return moved(own_hbm, outer, row_piece(c, coarse, low), lo_s.at[c], lo_r.at[c], 1)

    def first_on(src, c, target):
        return moved(src, near, row_piece(c, fine, high), nr_s.at[c], nr_r.at[c], target)

    def second_on(src, c, target):
        return moved(src, far, row_piece(c, fine, high), fr_s.at[c], fr_r.at[c], target)

    def second_last(n):
        where = row_piece(fine - 1, fine, lasts[n])
        m = fine - 1 + n
        return moved(own_hbm, far, where, fr_s.at[m], fr_r.at[m], 2)

    def last_low(g):
        return moved(own_hbm, outer, block_piece(g, 1, low), lo_s.at[g], lo_r.at[g], 2)

    def last_high(g):
        return moved(own_hbm, outer, block_piece(g, 1, high), hi_s.at[g], hi_r.at[g], 2)

    def last_on(g):
        return moved(outer, far, block_piece(g, 1, low), fl_s.at[g], fl_r.at[g], 1)

    def third_on(src, g, target):
        return moved(src, near, block_piece(g, 1, low), mid_s.at[g], mid_r.at[g], target)

    def share(slot, piece, where):
        copies = []
        for d in range(1, groups):
            other = lax.rem(me + d, groups)
            copies.append(
                pltpu.make_async_remote_copy(
                    src_ref=stage.at[(slot, other) + where],
                    dst_ref=inbox.at[(slot, d - 1) + where],
                    send_sem=rs_s.at[slot, piece, d - 1],
                    recv_sem=rs_r.at[slot, piece, d - 1],
                    device_id={"ell": other // pols, "pol": lax.rem(other, pols)},
                    device_id_type=pl.DeviceIdType.MESH,
                )
            )
        return copies

    def start_share(slot, piece, where):
        for copy in share(slot, piece, where):
            copy.start()

    def rows_of(c, pieces):
        return (every, span(c, pieces), every)

    def cols_of(g, count=1):
        size = count * rows
        return (every, every, pl.ds(pl.multiple_of(g * size, size), size))

    def wide_cols(g):
        return cols_of(g, held)

    def dot(a, b):
        return lax.dot_general(a, b, (((1,), (1,)), ((), ())), preferred_element_type=f32)

    def product(left, left_where, weight, right, right_where):
        def scaled(part_index):
            value = left[(part_index,) + left_where].reshape(-1, weight.shape[-1])
            return (weight * value.astype(f32)).astype(bf16)

        a_re, a_im = scaled(0), scaled(1)
        b_re = right[(0,) + right_where].reshape(-1, weight.shape[-1])
        b_im = right[(1,) + right_where].reshape(-1, weight.shape[-1])
        both = dot(jnp.concatenate([a_re, a_im], 0), b_re)
        return both + dot(jnp.concatenate([a_im, -a_re], 0), b_im)

    def cross(*operands):
        both = product(*operands)
        size = both.shape[0] // 2
        return both[:size].astype(bf16), both[size:].astype(bf16)

    def row_operands(c, pieces, left, weights, sep, right, part):
        return (
            left, (every, span(c, pieces), lanes(part)), weights[sep, :, lanes(part)],
            right, (every, every, lanes(part)),
        )

    def by_rows(slot, c, pieces, *rest):
        put_rows(slot, c, pieces, *cross(*row_operands(c, pieces, *rest)))
        start_share(slot, c, rows_of(c, pieces))

    def put_rows(slot, c, pieces, real, imag):
        stage[slot, :, 0, span(c, pieces), :] = real.reshape(groups, rows // pieces, modes)
        stage[slot, :, 1, span(c, pieces), :] = imag.reshape(groups, rows // pieces, modes)

    def column_product(o, g, count, left, weights, sep, right, part):
        return product(
            left, (pl.ds(o * held, held), every, lanes(part)), weights[sep, :, lanes(part)],
            right, (pl.ds(g * count, count), every, lanes(part)),
        )

    def by_columns(slot, g, count, *operands, base=None):
        columns = cols_of(g, count)[-1]

        def body(o):
            both = column_product(o, g, count, *operands)
            both = both if base is None else both + base[o]
            size = both.shape[0] // 2
            real, imag = both[:size].astype(bf16), both[size:].astype(bf16)
            stage[slot, pl.ds(o * held, held), 0, :, columns] = real.reshape(held, rows, -1)
            stage[slot, pl.ds(o * held, held), 1, :, columns] = imag.reshape(held, rows, -1)

        loop(0, halves, body)
        start_share(slot, g, cols_of(g, count))

    def await_share(slot, piece, where):
        for copy in share(slot, piece, where):
            copy.wait_recv()

    def added(slot, where):
        total = stage[(slot, me) + where].astype(f32)
        for d in range(groups - 1):
            total = total + inbox[(slot, d) + where].astype(f32)
        return total

    def settle(slot, pieces, where_of, lo=0):
        def body(c):
            for copy in share(slot, c, where_of(c)):
                copy.wait_send()

        loop(lo, pieces, body)

    def fine_rows(c):
        return rows_of(c, fine)

    def coarse_rows(c):
        return rows_of(c, coarse)

    def give_back(slot, c):
        where = fine_rows(c)
        return to_freq(
            back_out.at[(slot,) + where], back_in.at[(slot,) + where],
            bk_s.at[slot, c], bk_r.at[slot, c], 0 if slot in (S0, S3) else 1,
        )

    def returned(slot):
        def body(c):
            where = fine_rows(c)
            await_share(slot, c, where)
            back_out[(slot,) + where] = added(slot, where).astype(bf16)
            give_back(slot, c).start()

        return body

    def paired(slot):
        where = fine_rows(fine - 1)
        return [
            pltpu.make_async_remote_copy(
                src_ref=stage.at[(slot, e * pols + 1 - core) + where],
                dst_ref=inbox.at[(slot, e) + where],
                send_sem=rs_s.at[slot, fine - 1, e], recv_sem=rs_r.at[slot, fine - 1, e],
                device_id={"pol": 1 - core}, device_id_type=pl.DeviceIdType.MESH,
            )
            for e in range(groups // pols)
        ]

    def pair_on(n, e, origin):
        return pltpu.make_async_remote_copy(
            src_ref=pair_out.at[n, e], dst_ref=pair_in.at[n, origin],
            send_sem=pair_s.at[n, e], recv_sem=pair_r.at[n, origin],
            device_id={"freq": 1, "ell": e}, device_id_type=pl.DeviceIdType.MESH,
        )

    def pairs_sent(n, slot):
        where = fine_rows(fine - 1)
        for copy in paired(slot):
            copy.wait_recv()
        for e in range(groups // pols):
            total = stage[(slot, e * pols + core) + where].astype(f32)
            total = total + inbox[(slot, e) + where].astype(f32)
            pair_out[n, e] = total.astype(bf16)
        pair_on(n, 1 - line, line).start()
        pair_on(n, line, line).start()

    def deliver(n, c):
        where = coarse_rows(c)
        return to_freq(
            final_out.at[(n,) + where], final_in.at[(n,) + where], fn_s.at[n, c], fn_r.at[n, c], 0
        )

    def delivered(slot, n):
        def body(c):
            where = coarse_rows(c)
            await_share(slot, c, where)
            final_out[(n,) + where] = added(slot, where).astype(bf16)
            deliver(n, c).start()

        return body

    def finish(sep, first_row, count, first_block, total):
        weight = taper[sep, pl.ds(first_row, count), pl.ds(first_block * LANES, total.shape[-1])]
        weight = weight.astype(f32)
        for part in range(2):
            value = weight * total[part]
            for j in range(total.shape[-1] // LANES):
                start = first_row * per_row + 2 * (first_block + j) + part
                out[sep, pl.ds(start, count, stride=per_row), :] = value[
                    :, j * LANES:(j + 1) * LANES
                ]

    def add_noise(sep, first_row, count):
        where = pl.ds(first_row * per_row, count * per_row)
        out[sep, where, :] = out[sep, where, :] + noise[sep, where, :].astype(f32)

    def finish_rows(sep, c, pieces, total):
        step = rows // pieces
        first_row = pl.multiple_of(c * step, step)
        finish(sep, first_row, step, 0, total)
        add_noise(sep, first_row, step)

    def clear(sep):
        out[sep] = noise[sep].astype(f32)

    @pl.when(freq == 0)
    def _():
        outer_high(0).start()
        first_rows(1).start()
        loop(1, fine, lambda c: outer_high(c).start())
        loop(0, coarse, lambda c: outer_low(c).start())
        loading.wait()
        spectra.wait()
        tapers.wait()
        noises.wait()
        loop(0, groups, lambda g: third_on(near, g, 0).wait_recv())
        loop(0, coarse, lambda c: by_rows(S0, c, coarse, own, spec, 1, near, low))
        loop(0, coarse, lambda c: await_share(S0, c, coarse_rows(c)))

        def ends(c):
            deliver(0, c).wait_recv()
            finish_rows(0, c, coarse, final_in[(0,) + coarse_rows(c)].astype(f32))

        def middles(c):
            where = fine_rows(c)
            give_back(S0, c).wait_recv()
            finish_rows(1, c, fine, added(S0, where) + back_in[(S0,) + where].astype(f32))

        def longs(c):
            per = fine // coarse
            where = fine_rows(c)

            @pl.when(lax.rem(c, per) == 0)
            def _():
                deliver(1, c // per).wait_recv()

            give_back(S3, c).wait_recv()
            total = final_in[(1,) + where].astype(f32) + back_in[(S3,) + where].astype(f32)
            finish_rows(2, c, fine, total)

        loop(0, coarse - 1, ends)
        loop(0, fine, middles)
        loop(coarse - 1, coarse, ends)
        loop(0, fine, longs)
        first_rows(1).wait_send()
        loop(0, fine, lambda c: outer_high(c).wait_send())
        loop(0, coarse, lambda c: outer_low(c).wait_send())
        settle(S0, coarse, coarse_rows)

    @pl.when(freq == 1)
    def _():
        second_on(own_hbm, 0, 2).start()
        second_rows(2).start()
        loop(1, LEAD, lambda c: second_on(own_hbm, c, 2).start())
        first_rows(1).wait_recv()
        first_rows(2).start()

        def relay(c):
            outer_high(c).wait_recv()
            first_on(outer, c, 2).start()

        def relay_back(g):
            third_on(own_hbm, g, 1).wait_recv()
            third_on(near, g, 0).start()

        done = 0
        for c in range(fine):
            relay(c)
            while done < groups and 2 * fine * (done + 1) <= groups * (2 * c + 3):
                relay_back(done)
                done += 1
        for g in range(done, groups):
            relay_back(g)
        loop(LEAD, fine - 1, lambda c: second_on(own_hbm, c, 2).start())
        for n in range(2):
            second_last(n).start()
        loading.wait()
        spectra.wait()
        tapers.wait()
        noises.wait()
        clear(2)
        loop(0, coarse, lambda c: by_rows(S1, c, coarse, own, spec, 0, near, low))

        def take(c):
            outer_low(c).wait_recv()
            by_rows(S0, c, coarse, outer, spec0, 0, own, full)

            @pl.when(c == 0)
            def _():
                loop(0, held, lambda g: last_on(g).wait_recv())
                by_columns(S2, 0, held, own, spec, 1, far, low)

            @pl.when(c == coarse - 2)
            def _():
                loop(held, groups, lambda g: last_on(g).wait_recv())

            @pl.when(c >= coarse - 2)
            def _():
                loop(
                    jnp.where(c == coarse - 2, 0, c), c + 1,
                    lambda r: by_rows(S3, r, coarse, outer, spec0, 2, far, low),
                )

            loop(jnp.maximum(c - 1, 0), c, delivered(S0, 0))
            loop(0, jnp.where(c == coarse - 1, c, 0), delivered(S3, 1))

        loop(0, coarse, take)
        loop(1, halves, lambda g: by_columns(S2, g, held, own, spec, 1, far, low))
        loop(coarse - 1, coarse, delivered(S0, 0))
        loop(coarse - 1, coarse, delivered(S3, 1))
        loop(0, coarse, lambda c: await_share(S1, c, coarse_rows(c)))

        def ends(slot, sep):
            def body(c):
                where = fine_rows(c)
                give_back(slot, c).wait_recv()
                finish_rows(sep, c, fine, added(slot, where) + back_in[(slot,) + where].astype(f32))

            return body

        loop(0, few, ends(S1, 0))
        loop(0, halves, lambda g: await_share(S2, g, wide_cols(g)))
        loop(0, few, ends(S2, 1))

        def late(c):
            ends(S1, 0)(c)
            ends(S2, 1)(c)

        second_rows(2).wait_send()
        first_rows(2).wait_send()
        loop(0, fine - 1, lambda c: second_on(own_hbm, c, 2).wait_send())
        for n in range(2):
            second_last(n).wait_send()
        loop(0, fine, lambda c: first_on(outer, c, 2).wait_send())
        loop(0, groups, lambda g: third_on(near, g, 0).wait_send())
        for slot in (S0, S1, S3):
            settle(slot, coarse, coarse_rows)
        settle(S2, halves, wide_cols)
        for n in range(2):
            loop(0, coarse, lambda c: deliver(n, c).wait_send())
        loop(few, fine - 1, late)
        where = fine_rows(fine - 1)
        for n, slot in enumerate((S1, S2)):
            total = added(slot, where)
            for e in range(groups // pols):
                pair_on(n, line, e).wait_recv()
                total = total + pair_in[n, e].astype(f32)
            finish_rows(n, fine - 1, fine, total)

    @pl.when(freq == 2)
    def _():
        loop(0, groups, lambda g: third_on(own_hbm, g, 1).start())
        loading.wait()
        spectra.wait()
        tapers.wait()
        noises.wait()
        clear(1)
        clear(2)
        second_rows(2).wait_recv()
        second_rows(3).start()

        def second(c):
            second_on(own_hbm, c, 2).wait_recv()
            second_on(far, c, 3).start()
            by_rows(S1, c, fine, far, spec1, 0, own, high)

        def first(c):
            first_on(outer, c, 2).wait_recv()
            first_on(near, c, 3).start()

            g = c // gap

            @pl.when(jnp.logical_and(lax.rem(c, gap) == 0, g < groups))
            def _():
                last_low(g).wait_recv()
                last_on(g).start()

            by_rows(S0, c, fine, near, spec0, 1, own, high)
            loop(0, jnp.where(c == settled, LEAD, 0), returned(S1))
            before = jnp.where(c == settled, 0, jnp.maximum(c - 1, 0))
            loop(before, jnp.where(c >= settled, c, before), returned(S0))

        def block(g):
            by_columns(S3, g, 1, own, spec, 0, outer, full)

        def block_in(g):
            last_high(g).wait_recv()

        def last_base(o):
            base[o] = column_product(o, groups - 1, 1, own, spec, 0, outer, low)

        def last_block(g):
            by_columns(S3, g, 1, own, spec, 0, outer, high, base=base)

        loop(0, LEAD, second)
        first_rows(2).wait_recv()
        first_rows(3).start()
        loop(0, fine, first)

        def second_more(c):
            second(c)
            loop(c - 1, jnp.where(c > LEAD, c, c - 1), returned(S1))
            loop(fine - 1, jnp.where(c == LEAD, fine, fine - 1), returned(S0))
            g = jnp.where(c < LEAD + gap, 0, jnp.where(c < few - gap, 1, 2))
            due = jnp.logical_or(c == LEAD, jnp.logical_or(c == LEAD + gap, c == few - gap))
            loop(g, jnp.where(due, g + 1, g), block_in)
            loop(g, jnp.where(due, g + 1, g), block)

        loop(0, halves, last_base)
        loop(LEAD, few, second_more)
        loop(few - 1, few, returned(S1))

        def late(c):
            second_on(own_hbm, c, 2).wait_recv()
            by_rows(S1, c, fine, far, spec1, 0, own, high)
            loop(groups - 1, jnp.where(c == few, groups, groups - 1), block_in)
            by_rows(S2, c, fine, far, spec1, 1, outer, high)
            loop(groups - 1, jnp.where(c == few, groups, groups - 1), last_block)

        loop(few, fine - 1, late)
        c = fine - 1
        ways = ((S1, own), (S2, outer))
        loop(few, c, returned(S1))
        second_last(0).wait_recv()
        for n, (slot, right) in enumerate(ways):
            held_sum[n] = product(*row_operands(c, fine, far, spec1, n, right, lasts[0]))
        loop(few, c, returned(S2))
        second_last(1).wait_recv()
        for n, (slot, right) in enumerate(ways):
            both = held_sum[n] + product(*row_operands(c, fine, far, spec1, n, right, lasts[1]))
            size = both.shape[0] // 2
            put_rows(slot, c, fine, both[:size].astype(bf16), both[size:].astype(bf16))
            for copy in paired(slot):
                copy.start()
        pairs_sent(0, S1)
        pairs_sent(1, S2)
        for g in range(groups):
            where = cols_of(g)
            await_share(S3, g, where)
            finish(0, 0, rows, g * rows // LANES, added(S3, where))
        add_noise(0, 0, rows)

        second_rows(3).wait_send()
        first_rows(3).wait_send()
        loop(0, groups, lambda g: third_on(own_hbm, g, 1).wait_send())
        loop(0, groups, lambda g: last_on(g).wait_send())
        loop(0, fine, lambda c: first_on(near, c, 3).wait_send())
        loop(0, few, lambda c: second_on(far, c, 3).wait_send())
        settle(S0, fine, fine_rows)
        settle(S1, fine - 1, fine_rows)
        settle(S2, fine - 1, fine_rows, few)
        for n, slot in enumerate((S1, S2)):
            for copy in paired(slot):
                copy.wait_send()
            for e in range(groups // pols):
                pair_on(n, e, line).wait_send()
        settle(S3, groups, cols_of)
        loop(0, fine, lambda c: give_back(S0, c).wait_send())
        loop(0, fine - 1, lambda c: give_back(S1, c).wait_send())
        loop(few, fine - 1, lambda c: give_back(S2, c).wait_send())

    @pl.when(freq == 3)
    def _():
        loop(0, groups, lambda g: last_low(g).start())
        loading.wait()
        spectra.wait()
        tapers.wait()
        noises.wait()
        for sep in range(3):
            clear(sep)
        second_rows(3).wait_recv()

        def second(c):
            second_on(far, c, 3).wait_recv()
            by_rows(S2, c, fine, far, spec1, 1, own, high)
            returned(S2)(c)

        def first(c):
            first_on(near, c, 3).wait_recv()
            by_rows(S3, c, fine, near, spec0, 2, own, high)
            returned(S3)(c)
            loop(held, jnp.where(c == fine - groups, groups, held), lambda g: last_high(g).start())

        loop(0, LEAD, second)
        loop(0, held, lambda g: last_high(g).start())
        first_rows(3).wait_recv()
        loop(0, fine, first)
        loop(LEAD, few, second)
        loop(0, groups, lambda g: last_low(g).wait_send())
        loop(0, groups, lambda g: last_high(g).wait_send())
        settle(S3, fine, fine_rows)
        settle(S2, few, fine_rows)
        loop(0, fine, lambda c: give_back(S3, c).wait_send())
        loop(0, few, lambda c: give_back(S2, c).wait_send())


def meet_covariance(beam_matrix, sky_spectrum, taper_tiles, noise_tiles):
    _, parts, modes, width = beam_matrix.shape
    separations, local_rows, _ = taper_tiles.shape
    groups = modes // local_rows
    tiles = 4 * 2 * local_rows * modes
    block = parts * modes * width
    cut = int(width * (0.5 - tiles / (4 * block))) // LANES * LANES
    bf16, f32 = jnp.bfloat16, jnp.float32
    shape = (parts, groups, local_rows, width)
    tile = (2, local_rows, modes)
    blocks = modes // LANES
    dma = pltpu.SemaphoreType.DMA
    pair = lambda *dims: [dma(dims), dma(dims)]
    vmem = pl.BlockSpec(memory_space=pltpu.VMEM)
    hbm = pl.BlockSpec(memory_space=pltpu.HBM)
    spec = jnp.swapaxes(sky_spectrum, 0, 1)
    noise = noise_tiles.reshape(separations, local_rows, 2, blocks, LANES)
    noise = jnp.swapaxes(noise, 2, 3).reshape(separations, -1, LANES)
    kept = lambda array: pltpu.with_memory_space_constraint(array, pltpu.HBM)
    lines = pl.pallas_call(
        functools.partial(meet_kernel, cut),
        out_shape=jax.ShapeDtypeStruct((separations, local_rows * blocks * 2, LANES), f32),
        in_specs=[hbm, hbm, hbm, hbm],
        out_specs=vmem,
        scratch_shapes=[
            pltpu.VMEM(shape, bf16), pltpu.VMEM(spec.shape, f32),
            pltpu.VMEM(taper_tiles.shape, bf16), pltpu.VMEM(noise.shape, bf16),
            *[pltpu.VMEM(shape, bf16)] * 3,
            *[pltpu.VMEM(spec.shape, f32)] * 2,
            pltpu.VMEM((4, groups) + tile, bf16),
            pltpu.VMEM((4, groups - 1) + tile, bf16),
            *[pltpu.VMEM((4,) + tile, bf16)] * 2,
            *[pltpu.VMEM((2,) + tile, bf16)] * 2,
            pltpu.VMEM((2, 2 * modes // FINE, modes), f32),
            pltpu.VMEM((2, modes, local_rows), f32),
            *[pltpu.VMEM((2, 2, 2, local_rows // FINE, modes), bf16)] * 2,
            dma, dma, dma, dma, *pair(5), *pair(FINE), *pair(max(COARSE, groups)), *pair(groups),
            *pair(FINE), *pair(FINE + 1), *pair(groups),
            *pair(4, FINE, groups - 1), *pair(4, FINE), *pair(2, COARSE), *pair(2, 2),
        ],
        compiler_params=pltpu.CompilerParams(
            collective_id=0, has_side_effects=True, vmem_limit_bytes=51 * 2**20,
        ),
    )(kept(beam_matrix[0].reshape(shape)), kept(spec), kept(taper_tiles), kept(noise))
    lines = lines.reshape(1, separations, local_rows, blocks, 2, LANES)
    return jnp.swapaxes(lines, 3, 4).reshape(1, separations, local_rows, 2, modes)


def local(beam_matrix, sky_spectrum, taper_tiles, noise_tiles):
    per_device, _, modes, width = beam_matrix.shape
    separations = sky_spectrum.shape[1]
    local_rows = taper_tiles.shape[1]
    in_line = (
        per_device == 1
        and separations == 3
        and lax.axis_size("freq") == separations + 1
        and modes // local_rows == 4
        and lax.axis_size("pol") == 2
        and local_rows % LANES == 0
        and width % (8 * LANES) == 0
    )
    if in_line:
        return meet_covariance(beam_matrix, sky_spectrum, taper_tiles, noise_tiles)
    summed = general_sums(beam_matrix, sky_spectrum, local_rows)
    summed = summed.reshape(per_device, separations, local_rows, 2, modes)
    taper = taper_tiles.astype(jnp.float32)[None, :, :, None, :]
    return taper * summed + noise_tiles.astype(jnp.float32)


def solution(mesh):
    placed = (
        P(("grp", "freq"), None, None, ("ell", "pol")),
        P(("grp", "freq"), None, ("ell", "pol")),
        P(None, ("ell", "pol"), None),
        P(("grp", "freq"), None, ("ell", "pol"), None, None),
    )
    return jax.shard_map(
        local,
        mesh=mesh,
        in_specs=placed,
        out_specs=P(("grp", "freq"), None, ("ell", "pol"), None, None),
        check_vma=False,
    )
```

```python
import functools

import jax
import jax.numpy as jnp
from jax import lax
from jax.experimental import pallas as pl
from jax.experimental.pallas import tpu as pltpu
from jax.sharding import PartitionSpec as P

FINE = 8
COARSE = 4
LEAD = 2
LATE = 2
EDGE = 2
LANES = 128


def passed_along(block, axis, distance):
    devices = range(lax.axis_size(axis))
    route = [(i - distance, i) for i in devices if i - distance in devices]
    return lax.ppermute(block, axis, route)


def general_sums(beam_matrix, sky_spectrum, local_rows):
    per_device = beam_matrix.shape[0]
    mode_count = beam_matrix.shape[2]
    separations = sky_spectrum.shape[1]
    needed = (per_device - 1 + separations) // per_device
    blocks = [beam_matrix]
    for offset in range(needed):
        blocks.append(passed_along(beam_matrix, "freq", -(offset + 1)))
    term_list = []
    for sep_index in range(separations):
        target = sep_index + 1
        partner = blocks[target // per_device][target % per_device]
        spec_row = sky_spectrum[0, sep_index]
        scaled = (spec_row[None, None, :] * beam_matrix[0].astype(jnp.float32)).astype(jnp.bfloat16)
        right = jnp.concatenate([partner[0], partner[1]], axis=-1)
        top = jnp.concatenate([scaled[0], scaled[1]], axis=-1)
        bottom = jnp.concatenate([scaled[1], -scaled[0]], axis=-1)
        left = jnp.stack([top, bottom], axis=1).reshape(2 * mode_count, top.shape[-1])
        product = lax.dot_general(
            left, right, (((1,), (1,)), ((), ())), preferred_element_type=jnp.float32
        ).reshape(mode_count, 2, mode_count)
        term_list.append(
            lax.psum_scatter(
                product.astype(jnp.bfloat16), ("ell", "pol"), scatter_dimension=0, tiled=True
            ).astype(jnp.float32)
        )
    return jnp.stack(term_list)


S0, S1, S2, S3 = range(4)


def meet_kernel(
    cut, own_hbm, spec_hbm, taper_hbm, noise_hbm, out,
    own, spec, taper, noise, outer, near, far, spec0, spec1, stage, inbox, back_out, back_in, final_out, final_in, held_sum, base, pair_out, pair_in,
    load, load_spec, load_taper, load_noise, spec_s, spec_r, hi_s, hi_r, lo_s, lo_r, mid_s, mid_r, nr_s, nr_r, fr_s, fr_r, fl_s, fl_r,
    rs_s, rs_r, bk_s, bk_r, fn_s, fn_r, pair_s, pair_r,
):
    f32, bf16 = jnp.float32, jnp.bfloat16
    _, groups, rows, width = own.shape
    modes = groups * rows
    fine, coarse, halves = FINE, COARSE, 2
    held = groups // halves
    few = fine - LATE
    gap = fine // (groups + 1)
    settled = gap * (groups - 1) + 1
    freqs = lax.axis_size("freq")
    pols = lax.axis_size("pol")
    freq = lax.axis_index("freq")
    line, core = lax.axis_index("ell"), lax.axis_index("pol")
    me = line * pols + core
    low, high, full = (0, cut), (cut, width), (0, width)
    edge = width - EDGE * LANES
    lasts = ((cut, edge), (edge, width))
    every = slice(None)
    per_row = 2 * modes // LANES

    loading = pltpu.make_async_copy(own_hbm, own, load)
    loading.start()
    spectra = pltpu.make_async_copy(spec_hbm, spec, load_spec)
    spectra.start()
    tapers = pltpu.make_async_copy(taper_hbm, taper, load_taper)
    tapers.start()
    noises = pltpu.make_async_copy(noise_hbm, noise, load_noise)
    noises.start()

    barrier = pltpu.get_barrier_semaphore()
    @pl.when(freq > 0)
    def _():
        pl.semaphore_signal(
            barrier, inc=1, device_id={"freq": freq - 1}, device_id_type=pl.DeviceIdType.MESH
        )

    @pl.when(freq < freqs - 1)
    def _():
        pl.semaphore_signal(
            barrier, inc=1, device_id={"freq": freq + 1}, device_id_type=pl.DeviceIdType.MESH
        )

    for d in range(1, groups):
        other = lax.rem(me + d, groups)
        pl.semaphore_signal(
            barrier, inc=1, device_id={"ell": other // pols, "pol": lax.rem(other, pols)},
            device_id_type=pl.DeviceIdType.MESH,
        )
    beside = jnp.where(freq > 0, 1, 0) + jnp.where(freq < freqs - 1, 1, 0)
    pl.semaphore_wait(barrier, beside + groups - 1)

    def span(c, pieces):
        step = rows // pieces
        return pl.ds(pl.multiple_of(c * step, step), step)

    def to_freq(src, dst, send, recv, target):
        return pltpu.make_async_remote_copy(
            src_ref=src, dst_ref=dst, send_sem=send, recv_sem=recv,
            device_id={"freq": target}, device_id_type=pl.DeviceIdType.MESH,
        )

    def lanes(part):
        return pl.ds(part[0], part[1] - part[0])

    def loop(lo, hi, body):
        def wrapped(i, carry):
            body(i)
            return carry

        lax.fori_loop(lo, hi, wrapped, 0)

    def send_spec(src, dst, seps, part, n, target):
        where = (pl.ds(seps[0], len(seps)), every, lanes(part))
        return to_freq(src.at[where], dst.at[where], spec_s.at[n], spec_r.at[n], target)

    def first_rows(target):
        if target == 1:
            return send_spec(spec_hbm, spec0, (0, 1, 2), full, 0, 1)
        return send_spec(spec0, spec0, (1, 2) if target == 2 else (2,), high, target - 1, target)

    def second_rows(target):
        if target == 2:
            return send_spec(spec_hbm, spec1, (0, 1), high, 3, 2)
        return send_spec(spec1, spec1, (1,), high, 4, 3)

    def moved(src, dst, where, send, recv, target):
        return to_freq(src.at[where], dst.at[where], send, recv, target)

    def row_piece(c, pieces, part):
        return (every, every, span(c, pieces), lanes(part))

    def block_piece(g, count, part):
        return (every, pl.ds(g * count, count), every, lanes(part))

    def outer_high(c):
        return moved(own_hbm, outer, row_piece(c, fine, high), hi_s.at[c], hi_r.at[c], 1)

    def outer_low(c):
        return moved(own_hbm, outer, row_piece(c, coarse, low), lo_s.at[c], lo_r.at[c], 1)

    def first_on(src, c, target):
        return moved(src, near, row_piece(c, fine, high), nr_s.at[c], nr_r.at[c], target)

    def second_on(src, c, target):
        return moved(src, far, row_piece(c, fine, high), fr_s.at[c], fr_r.at[c], target)

    def second_last(n):
        where = row_piece(fine - 1, fine, lasts[n])
        m = fine - 1 + n
        return moved(own_hbm, far, where, fr_s.at[m], fr_r.at[m], 2)

    def last_low(g):
        return moved(own_hbm, outer, block_piece(g, 1, low), lo_s.at[g], lo_r.at[g], 2)

    def last_high(g):
        return moved(own_hbm, outer, block_piece(g, 1, high), hi_s.at[g], hi_r.at[g], 2)

    def last_on(g):
        return moved(outer, far, block_piece(g, 1, low), fl_s.at[g], fl_r.at[g], 1)

    def third_on(src, g, target):
        return moved(src, near, block_piece(g, 1, low), mid_s.at[g], mid_r.at[g], target)

    def share(slot, piece, where):
        copies = []
        for d in range(1, groups):
            other = lax.rem(me + d, groups)
            copies.append(
                pltpu.make_async_remote_copy(
                    src_ref=stage.at[(slot, other) + where],
                    dst_ref=inbox.at[(slot, d - 1) + where],
                    send_sem=rs_s.at[slot, piece, d - 1],
                    recv_sem=rs_r.at[slot, piece, d - 1],
                    device_id={"ell": other // pols, "pol": lax.rem(other, pols)},
                    device_id_type=pl.DeviceIdType.MESH,
                )
            )
        return copies

    def start_share(slot, piece, where):
        for copy in share(slot, piece, where):
            copy.start()

    def rows_of(c, pieces):
        return (every, span(c, pieces), every)

    def cols_of(g, count=1):
        size = count * rows
        return (every, every, pl.ds(pl.multiple_of(g * size, size), size))

    def wide_cols(g):
        return cols_of(g, held)

    def dot(a, b):
        return lax.dot_general(a, b, (((1,), (1,)), ((), ())), preferred_element_type=f32)

    def product(left, left_where, weight, right, right_where):
        def scaled(part_index):
            value = left[(part_index,) + left_where].reshape(-1, weight.shape[-1])
            return (weight * value.astype(f32)).astype(bf16)

        a_re, a_im = scaled(0), scaled(1)
        b_re = right[(0,) + right_where].reshape(-1, weight.shape[-1])
        b_im = right[(1,) + right_where].reshape(-1, weight.shape[-1])
        both = dot(jnp.concatenate([a_re, a_im], 0), b_re)
        return both + dot(jnp.concatenate([a_im, -a_re], 0), b_im)

    def cross(*operands):
        both = product(*operands)
        size = both.shape[0] // 2
        return both[:size].astype(bf16), both[size:].astype(bf16)

    def row_operands(c, pieces, left, weights, sep, right, part):
        return (
            left, (every, span(c, pieces), lanes(part)), weights[sep, :, lanes(part)],
            right, (every, every, lanes(part)),
        )

    def by_rows(slot, c, pieces, *rest):
        put_rows(slot, c, pieces, *cross(*row_operands(c, pieces, *rest)))
        start_share(slot, c, rows_of(c, pieces))

    def put_rows(slot, c, pieces, real, imag):
        stage[slot, :, 0, span(c, pieces), :] = real.reshape(groups, rows // pieces, modes)
        stage[slot, :, 1, span(c, pieces), :] = imag.reshape(groups, rows // pieces, modes)

    def column_product(o, g, count, left, weights, sep, right, part):
        return product(
            left, (pl.ds(o * held, held), every, lanes(part)), weights[sep, :, lanes(part)],
            right, (pl.ds(g * count, count), every, lanes(part)),
        )

    def by_columns(slot, g, count, *operands, base=None):
        columns = cols_of(g, count)[-1]

        def body(o):
            both = column_product(o, g, count, *operands)
            both = both if base is None else both + base[o]
            size = both.shape[0] // 2
            real, imag = both[:size].astype(bf16), both[size:].astype(bf16)
            stage[slot, pl.ds(o * held, held), 0, :, columns] = real.reshape(held, rows, -1)
            stage[slot, pl.ds(o * held, held), 1, :, columns] = imag.reshape(held, rows, -1)

        loop(0, halves, body)
        start_share(slot, g, cols_of(g, count))

    def await_share(slot, piece, where):
        for copy in share(slot, piece, where):
            copy.wait_recv()

    def added(slot, where):
        total = stage[(slot, me) + where].astype(f32)
        for d in range(groups - 1):
            total = total + inbox[(slot, d) + where].astype(f32)
        return total

    def settle(slot, pieces, where_of, lo=0):
        def body(c):
            for copy in share(slot, c, where_of(c)):
                copy.wait_send()

        loop(lo, pieces, body)

    def fine_rows(c):
        return rows_of(c, fine)

    def coarse_rows(c):
        return rows_of(c, coarse)

    def give_back(slot, c):
        where = fine_rows(c)
        return to_freq(
            back_out.at[(slot,) + where], back_in.at[(slot,) + where],
            bk_s.at[slot, c], bk_r.at[slot, c], 0 if slot in (S0, S3) else 1,
        )

    def returned(slot):
        def body(c):
            where = fine_rows(c)
            await_share(slot, c, where)
            back_out[(slot,) + where] = added(slot, where).astype(bf16)
            give_back(slot, c).start()

        return body

    def paired(slot):
        where = fine_rows(fine - 1)
        return [
            pltpu.make_async_remote_copy(
                src_ref=stage.at[(slot, e * pols + 1 - core) + where],
                dst_ref=inbox.at[(slot, e) + where],
                send_sem=rs_s.at[slot, fine - 1, e], recv_sem=rs_r.at[slot, fine - 1, e],
                device_id={"pol": 1 - core}, device_id_type=pl.DeviceIdType.MESH,
            )
            for e in range(groups // pols)
        ]

    def pair_on(n, e, origin):
        return pltpu.make_async_remote_copy(
            src_ref=pair_out.at[n, e], dst_ref=pair_in.at[n, origin],
            send_sem=pair_s.at[n, e], recv_sem=pair_r.at[n, origin],
            device_id={"freq": 1, "ell": e}, device_id_type=pl.DeviceIdType.MESH,
        )

    def pairs_sent(n, slot):
        where = fine_rows(fine - 1)
        for copy in paired(slot):
            copy.wait_recv()
        for e in range(groups // pols):
            total = stage[(slot, e * pols + core) + where].astype(f32)
            total = total + inbox[(slot, e) + where].astype(f32)
            pair_out[n, e] = total.astype(bf16)
        pair_on(n, 1 - line, line).start()

    def deliver(n, c):
        where = coarse_rows(c)
        return to_freq(
            final_out.at[(n,) + where], final_in.at[(n,) + where], fn_s.at[n, c], fn_r.at[n, c], 0
        )

    def delivered(slot, n):
        def body(c):
            where = coarse_rows(c)
            await_share(slot, c, where)
            final_out[(n,) + where] = added(slot, where).astype(bf16)
            deliver(n, c).start()

        return body

    def finish(sep, first_row, count, first_block, total):
        weight = taper[sep, pl.ds(first_row, count), pl.ds(first_block * LANES, total.shape[-1])]
        weight = weight.astype(f32)
        for part in range(2):
            value = weight * total[part]
            for j in range(total.shape[-1] // LANES):
                start = first_row * per_row + 2 * (first_block + j) + part
                out[sep, pl.ds(start, count, stride=per_row), :] = value[
                    :, j * LANES:(j + 1) * LANES
                ]

    def add_noise(sep, first_row, count):
        where = pl.ds(first_row * per_row, count * per_row)
        out[sep, where, :] = out[sep, where, :] + noise[sep, where, :].astype(f32)

    def finish_rows(sep, c, pieces, total):
        step = rows // pieces
        first_row = pl.multiple_of(c * step, step)
        finish(sep, first_row, step, 0, total)
        add_noise(sep, first_row, step)

    def clear(sep):
        out[sep] = noise[sep].astype(f32)

    @pl.when(freq == 0)
    def _():
        outer_high(0).start()
        first_rows(1).start()
        loop(1, fine, lambda c: outer_high(c).start())
        loop(0, coarse, lambda c: outer_low(c).start())
        loading.wait()
        spectra.wait()
        tapers.wait()
        noises.wait()
        loop(0, groups, lambda g: third_on(near, g, 0).wait_recv())
        loop(0, coarse, lambda c: by_rows(S0, c, coarse, own, spec, 1, near, low))
        loop(0, coarse, lambda c: await_share(S0, c, coarse_rows(c)))

        def ends(c):
            deliver(0, c).wait_recv()
            finish_rows(0, c, coarse, final_in[(0,) + coarse_rows(c)].astype(f32))

        def middles(c):
            where = fine_rows(c)
            give_back(S0, c).wait_recv()
            finish_rows(1, c, fine, added(S0, where) + back_in[(S0,) + where].astype(f32))

        def longs(c):
            per = fine // coarse
            where = fine_rows(c)

            @pl.when(lax.rem(c, per) == 0)
            def _():
                deliver(1, c // per).wait_recv()

            give_back(S3, c).wait_recv()
            total = final_in[(1,) + where].astype(f32) + back_in[(S3,) + where].astype(f32)
            finish_rows(2, c, fine, total)

        loop(0, coarse - 1, ends)
        loop(0, fine, middles)
        loop(coarse - 1, coarse, ends)
        loop(0, fine, longs)
        first_rows(1).wait_send()
        loop(0, fine, lambda c: outer_high(c).wait_send())
        loop(0, coarse, lambda c: outer_low(c).wait_send())
        settle(S0, coarse, coarse_rows)

    @pl.when(freq == 1)
    def _():
        second_on(own_hbm, 0, 2).start()
        second_rows(2).start()
        loop(1, LEAD, lambda c: second_on(own_hbm, c, 2).start())
        first_rows(1).wait_recv()
        first_rows(2).start()

        def relay(c):
            outer_high(c).wait_recv()
            first_on(outer, c, 2).start()

        def relay_back(g):
            third_on(own_hbm, g, 1).wait_recv()
            third_on(near, g, 0).start()

        done = 0
        for c in range(fine):
            relay(c)
            while done < groups and 2 * fine * (done + 1) <= groups * (2 * c + 3):
                relay_back(done)
                done += 1
        for g in range(done, groups):
            relay_back(g)
        loop(LEAD, fine - 1, lambda c: second_on(own_hbm, c, 2).start())
        for n in range(2):
            second_last(n).start()
        loading.wait()
        spectra.wait()
        tapers.wait()
        noises.wait()
        clear(2)
        loop(0, coarse, lambda c: by_rows(S1, c, coarse, own, spec, 0, near, low))

        def take(c):
            outer_low(c).wait_recv()
            by_rows(S0, c, coarse, outer, spec0, 0, own, full)

            @pl.when(c == 0)
            def _():
                loop(0, held, lambda g: last_on(g).wait_recv())
                by_columns(S2, 0, held, own, spec, 1, far, low)

            @pl.when(c == coarse - 2)
            def _():
                loop(held, groups, lambda g: last_on(g).wait_recv())

            @pl.when(c >= coarse - 2)
            def _():
                loop(
                    jnp.where(c == coarse - 2, 0, c), c + 1,
                    lambda r: by_rows(S3, r, coarse, outer, spec0, 2, far, low),
                )

            loop(jnp.maximum(c - 1, 0), c, delivered(S0, 0))
            loop(0, jnp.where(c == coarse - 1, c, 0), delivered(S3, 1))

        loop(0, coarse, take)
        loop(1, halves, lambda g: by_columns(S2, g, held, own, spec, 1, far, low))
        loop(coarse - 1, coarse, delivered(S0, 0))
        loop(coarse - 1, coarse, delivered(S3, 1))
        loop(0, coarse, lambda c: await_share(S1, c, coarse_rows(c)))

        def ends(slot, sep):
            def body(c):
                where = fine_rows(c)
                give_back(slot, c).wait_recv()
                finish_rows(sep, c, fine, added(slot, where) + back_in[(slot,) + where].astype(f32))

            return body

        loop(0, few, ends(S1, 0))
        loop(0, halves, lambda g: await_share(S2, g, wide_cols(g)))
        loop(0, few, ends(S2, 1))

        def late(c):
            ends(S1, 0)(c)
            ends(S2, 1)(c)

        second_rows(2).wait_send()
        first_rows(2).wait_send()
        loop(0, fine - 1, lambda c: second_on(own_hbm, c, 2).wait_send())
        for n in range(2):
            second_last(n).wait_send()
        loop(0, fine, lambda c: first_on(outer, c, 2).wait_send())
        loop(0, groups, lambda g: third_on(near, g, 0).wait_send())
        for slot in (S0, S1, S3):
            settle(slot, coarse, coarse_rows)
        settle(S2, halves, wide_cols)
        for n in range(2):
            loop(0, coarse, lambda c: deliver(n, c).wait_send())
        loop(few, fine - 1, late)
        where = fine_rows(fine - 1)
        for n, slot in enumerate((S1, S2)):
            total = added(slot, where)
            for e in range(groups // pols):
                pair_on(n, line, e).wait_recv()
                total = total + pair_in[n, e].astype(f32)
            finish_rows(n, fine - 1, fine, total)

    @pl.when(freq == 2)
    def _():
        loop(0, groups, lambda g: third_on(own_hbm, g, 1).start())
        loading.wait()
        spectra.wait()
        tapers.wait()
        noises.wait()
        clear(1)
        clear(2)
        second_rows(2).wait_recv()
        second_rows(3).start()

        def second(c):
            second_on(own_hbm, c, 2).wait_recv()
            second_on(far, c, 3).start()
            by_rows(S1, c, fine, far, spec1, 0, own, high)

        def first(c):
            first_on(outer, c, 2).wait_recv()
            first_on(near, c, 3).start()

            g = c // gap

            @pl.when(jnp.logical_and(lax.rem(c, gap) == 0, g < groups))
            def _():
                last_low(g).wait_recv()
                last_on(g).start()

            by_rows(S0, c, fine, near, spec0, 1, own, high)
            loop(0, jnp.where(c == settled, LEAD, 0), returned(S1))
            before = jnp.where(c == settled, 0, jnp.maximum(c - 1, 0))
            loop(before, jnp.where(c >= settled, c, before), returned(S0))

        def block(g):
            by_columns(S3, g, 1, own, spec, 0, outer, full)

        def block_in(g):
            last_high(g).wait_recv()

        def last_base(o):
            base[o] = column_product(o, groups - 1, 1, own, spec, 0, outer, low)

        def last_block(g):
            by_columns(S3, g, 1, own, spec, 0, outer, high, base=base)

        loop(0, LEAD, second)
        first_rows(2).wait_recv()
        first_rows(3).start()
        loop(0, fine, first)

        def second_more(c):
            second(c)
            loop(c - 1, jnp.where(c > LEAD, c, c - 1), returned(S1))
            loop(fine - 1, jnp.where(c == LEAD, fine, fine - 1), returned(S0))
            g = jnp.where(c < LEAD + gap, 0, jnp.where(c < few - gap, 1, 2))
            due = jnp.logical_or(c == LEAD, jnp.logical_or(c == LEAD + gap, c == few - gap))
            loop(g, jnp.where(due, g + 1, g), block_in)
            loop(g, jnp.where(due, g + 1, g), block)

        loop(0, halves, last_base)
        loop(LEAD, few, second_more)
        loop(few - 1, few, returned(S1))

        def late(c):
            second_on(own_hbm, c, 2).wait_recv()
            by_rows(S1, c, fine, far, spec1, 0, own, high)
            loop(groups - 1, jnp.where(c == few, groups, groups - 1), block_in)
            by_rows(S2, c, fine, far, spec1, 1, outer, high)
            loop(groups - 1, jnp.where(c == few, groups, groups - 1), last_block)

        loop(few, fine - 1, late)
        c = fine - 1
        ways = ((S1, own), (S2, outer))
        loop(few, c, returned(S1))
        second_last(0).wait_recv()
        for n, (slot, right) in enumerate(ways):
            held_sum[n] = product(*row_operands(c, fine, far, spec1, n, right, lasts[0]))
        loop(few, c, returned(S2))
        second_last(1).wait_recv()
        for n, (slot, right) in enumerate(ways):
            both = held_sum[n] + product(*row_operands(c, fine, far, spec1, n, right, lasts[1]))
            size = both.shape[0] // 2
            put_rows(slot, c, fine, both[:size].astype(bf16), both[size:].astype(bf16))
            for copy in paired(slot):
                copy.start()
        pairs_sent(0, S1)
        pairs_sent(1, S2)
        for n in range(2):
            pair_on(n, line, line).start()
        for g in range(groups):
            where = cols_of(g)
            await_share(S3, g, where)
            finish(0, 0, rows, g * rows // LANES, added(S3, where))
        add_noise(0, 0, rows)

        second_rows(3).wait_send()
        first_rows(3).wait_send()
        loop(0, groups, lambda g: third_on(own_hbm, g, 1).wait_send())
        loop(0, groups, lambda g: last_on(g).wait_send())
        loop(0, fine, lambda c: first_on(near, c, 3).wait_send())
        loop(0, few, lambda c: second_on(far, c, 3).wait_send())
        settle(S0, fine, fine_rows)
        settle(S1, fine - 1, fine_rows)
        settle(S2, fine - 1, fine_rows, few)
        for n, slot in enumerate((S1, S2)):
            for copy in paired(slot):
                copy.wait_send()
            for e in range(groups // pols):
                pair_on(n, e, line).wait_send()
        settle(S3, groups, cols_of)
        loop(0, fine, lambda c: give_back(S0, c).wait_send())
        loop(0, fine - 1, lambda c: give_back(S1, c).wait_send())
        loop(few, fine - 1, lambda c: give_back(S2, c).wait_send())

    @pl.when(freq == 3)
    def _():
        loop(0, groups, lambda g: last_low(g).start())
        loading.wait()
        spectra.wait()
        tapers.wait()
        noises.wait()
        for sep in range(3):
            clear(sep)
        second_rows(3).wait_recv()

        def second(c):
            second_on(far, c, 3).wait_recv()
            by_rows(S2, c, fine, far, spec1, 1, own, high)
            returned(S2)(c)

        def first(c):
            first_on(near, c, 3).wait_recv()
            by_rows(S3, c, fine, near, spec0, 2, own, high)
            returned(S3)(c)
            loop(held, jnp.where(c == fine - groups, groups, held), lambda g: last_high(g).start())

        loop(0, LEAD, second)
        loop(0, held, lambda g: last_high(g).start())
        first_rows(3).wait_recv()
        loop(0, fine, first)
        loop(LEAD, few, second)
        loop(0, groups, lambda g: last_low(g).wait_send())
        loop(0, groups, lambda g: last_high(g).wait_send())
        settle(S3, fine, fine_rows)
        settle(S2, few, fine_rows)
        loop(0, fine, lambda c: give_back(S3, c).wait_send())
        loop(0, few, lambda c: give_back(S2, c).wait_send())


def meet_covariance(beam_matrix, sky_spectrum, taper_tiles, noise_tiles):
    _, parts, modes, width = beam_matrix.shape
    separations, local_rows, _ = taper_tiles.shape
    groups = modes // local_rows
    tiles = 4 * 2 * local_rows * modes
    block = parts * modes * width
    cut = int(width * (0.5 - tiles / (4 * block))) // LANES * LANES
    bf16, f32 = jnp.bfloat16, jnp.float32
    shape = (parts, groups, local_rows, width)
    tile = (2, local_rows, modes)
    blocks = modes // LANES
    dma = pltpu.SemaphoreType.DMA
    pair = lambda *dims: [dma(dims), dma(dims)]
    vmem = pl.BlockSpec(memory_space=pltpu.VMEM)
    hbm = pl.BlockSpec(memory_space=pltpu.HBM)
    spec = jnp.swapaxes(sky_spectrum, 0, 1)
    noise = noise_tiles.reshape(separations, local_rows, 2, blocks, LANES)
    noise = jnp.swapaxes(noise, 2, 3).reshape(separations, -1, LANES)
    kept = lambda array: pltpu.with_memory_space_constraint(array, pltpu.HBM)
    lines = pl.pallas_call(
        functools.partial(meet_kernel, cut),
        out_shape=jax.ShapeDtypeStruct((separations, local_rows * blocks * 2, LANES), f32),
        in_specs=[hbm, hbm, hbm, hbm],
        out_specs=vmem,
        scratch_shapes=[
            pltpu.VMEM(shape, bf16), pltpu.VMEM(spec.shape, f32),
            pltpu.VMEM(taper_tiles.shape, bf16), pltpu.VMEM(noise.shape, bf16),
            *[pltpu.VMEM(shape, bf16)] * 3,
            *[pltpu.VMEM(spec.shape, f32)] * 2,
            pltpu.VMEM((4, groups) + tile, bf16),
            pltpu.VMEM((4, groups - 1) + tile, bf16),
            *[pltpu.VMEM((4,) + tile, bf16)] * 2,
            *[pltpu.VMEM((2,) + tile, bf16)] * 2,
            pltpu.VMEM((2, 2 * modes // FINE, modes), f32),
            pltpu.VMEM((2, modes, local_rows), f32),
            *[pltpu.VMEM((2, 2, 2, local_rows // FINE, modes), bf16)] * 2,
            dma, dma, dma, dma, *pair(5), *pair(FINE), *pair(max(COARSE, groups)), *pair(groups),
            *pair(FINE), *pair(FINE + 1), *pair(groups),
            *pair(4, FINE, groups - 1), *pair(4, FINE), *pair(2, COARSE), *pair(2, 2),
        ],
        compiler_params=pltpu.CompilerParams(
            collective_id=0, has_side_effects=True, vmem_limit_bytes=51 * 2**20,
        ),
    )(kept(beam_matrix[0].reshape(shape)), kept(spec), kept(taper_tiles), kept(noise))
    lines = lines.reshape(1, separations, local_rows, blocks, 2, LANES)
    return jnp.swapaxes(lines, 3, 4).reshape(1, separations, local_rows, 2, modes)


def local(beam_matrix, sky_spectrum, taper_tiles, noise_tiles):
    per_device, _, modes, width = beam_matrix.shape
    separations = sky_spectrum.shape[1]
    local_rows = taper_tiles.shape[1]
    in_line = (
        per_device == 1
        and separations == 3
        and lax.axis_size("freq") == separations + 1
        and modes // local_rows == 4
        and lax.axis_size("pol") == 2
        and local_rows % LANES == 0
        and width % (8 * LANES) == 0
    )
    if in_line:
        return meet_covariance(beam_matrix, sky_spectrum, taper_tiles, noise_tiles)
    summed = general_sums(beam_matrix, sky_spectrum, local_rows)
    summed = summed.reshape(per_device, separations, local_rows, 2, modes)
    taper = taper_tiles.astype(jnp.float32)[None, :, :, None, :]
    return taper * summed + noise_tiles.astype(jnp.float32)


def solution(mesh):
    placed = (
        P(("grp", "freq"), None, None, ("ell", "pol")),
        P(("grp", "freq"), None, ("ell", "pol")),
        P(None, ("ell", "pol"), None),
        P(("grp", "freq"), None, ("ell", "pol"), None, None),
    )
    return jax.shard_map(
        local,
        mesh=mesh,
        in_specs=placed,
        out_specs=P(("grp", "freq"), None, ("ell", "pol"), None, None),
        check_vma=False,
    )
```
